256 devices in a mesh: row: 16 (over z, core), col: 16 (over x, y).
Axes of the slice: x: 4, y: 4, z: 8, core: 2. Of those that a mesh axis runs over, the one named last changes fastest.
Arguments:
- matrix: float32 [12288, 12288], P('row', 'col'), may hold values from -40 to 40
Outputs:
- reduced: float32 [12288, 12288], P('row', 'col')
The draws below stay inside these ranges and needn't reach their ends.
All inputs are finite; a program needn't handle non-finite values.
Results may differ from the reference program's by a relative error of at most 0.00013.
Values sent between devices are 32-bit elements; how exact they have to be, the bound alone decides.
A program may use at most 128 MiB of HBM per device.

```python
import math
import jax
import jax.numpy as jnp
from jax import lax

BAND = 128
ORDER = 12288


def draw_matrix(key, part):
    noise_key, scale_key = jax.random.split(jax.random.fold_in(key, 11))
    noise = jnp.clip(jax.random.normal(noise_key, (ORDER, ORDER), jnp.float32), -4.0, 4.0)
    lowest, highest = (0.5, 2.0)
    scales = jnp.exp(jax.random.uniform(scale_key, (ORDER,), jnp.float32, math.log(lowest), math.log(highest)))
    symmetric = (noise + noise.T) * 0.5 ** 0.5
    return symmetric * scales[:, None] * scales[None, :]


def setup_inputs(seed: int = 0) -> dict:
    arg_keys = jax.random.split(jax.random.key(seed), 2)
    matrix = draw_matrix(jax.random.fold_in(arg_keys[1], 71), 0)
    return {"matrix": matrix}


HIGH = lax.Precision.HIGHEST

def matmul_plain(left, right):
    return jnp.dot(left, right, precision=HIGH, preferred_element_type=jnp.float32)

def inner_rows(left, right):
    return lax.dot_general(left, right, (((0,), (0,)), ((), ())), precision=HIGH, preferred_element_type=jnp.float32)

def outer_rows(left, right):
    return lax.dot_general(left, right, (((1,), (1,)), ((), ())), precision=HIGH, preferred_element_type=jnp.float32)

def join_blocks(top_left, top_right, bottom_left, bottom_right):
    return jnp.concatenate([jnp.concatenate([top_left, top_right], 1), jnp.concatenate([bottom_left, bottom_right], 1)], 0)

def lower_inverse(lower):
    size = lower.shape[0]
    identity = jnp.eye(size, dtype=jnp.float32)
    diag_vals = jnp.diagonal(lower)
    nilpotent = identity - lower / diag_vals[:, None]
    result = identity + nilpotent
    power = nilpotent
    reach = 2
    while reach < size:
        power = matmul_plain(power, power)
        result = result + matmul_plain(result, power)
        reach = reach * 2
    return result / diag_vals[None, :]

def upper_inverse_of(upper):
    return lower_inverse(upper.T).T

def cholesky_lower(gram):
    size = gram.shape[0]
    if size <= 8:
        positions = jnp.arange(size)
        current = gram
        columns_out = []
        for column in range(size):
            pivot = jnp.sqrt(current[column, column])
            column_vec = jnp.where(positions >= column, current[:, column] / pivot, 0.0)
            current = current - column_vec[:, None] * column_vec[None, :]
            columns_out.append(column_vec)
        return jnp.stack(columns_out, axis=1)
    half_size = size // 2
    top_low = cholesky_lower(gram[:half_size, :half_size])
    left_low = matmul_plain(gram[half_size:, :half_size], lower_inverse(top_low).T)
    bottom_low = cholesky_lower(gram[half_size:, half_size:] - outer_rows(left_low, left_low))
    zero_block = jnp.zeros((half_size, size - half_size), jnp.float32)
    return join_blocks(top_low, zero_block, left_low, bottom_low)

def unit_lu(square):
    size = square.shape[0]
    if size <= 8:
        identity = jnp.eye(size, dtype=jnp.float32)
        positions = jnp.arange(size)
        current = square
        lower_cols = []
        for column in range(size):
            ratios = jnp.where(positions > column, current[:, column] / current[column, column], 0.0)
            current = current - ratios[:, None] * current[column][None, :]
            lower_cols.append(ratios)
        lower = identity + jnp.stack(lower_cols, axis=1)
        upper = jnp.where(positions[:, None] <= positions[None, :], current, 0.0)
        return (lower, upper)
    half_size = size // 2
    lower_top, upper_top = unit_lu(square[:half_size, :half_size])
    upper_right = matmul_plain(lower_inverse(lower_top), square[:half_size, half_size:])
    lower_left = matmul_plain(square[half_size:, :half_size], upper_inverse_of(upper_top))
    schur_block = square[half_size:, half_size:] - matmul_plain(lower_left, upper_right)
    lower_bottom, upper_bottom = unit_lu(schur_block)
    zero_block = jnp.zeros((half_size, size - half_size), jnp.float32)
    lower = join_blocks(lower_top, zero_block, lower_left, lower_bottom)
    upper = join_blocks(upper_top, upper_right, zero_block.T, upper_bottom)
    return (lower, upper)

def factor(gram_sum, top_rows):
    size = gram_sum.shape[0]
    identity = jnp.eye(size, dtype=jnp.float32)
    cholesky_low = cholesky_lower(gram_sum)
    chol_inverse = lower_inverse(cholesky_low).T
    lower_f, upper_f = unit_lu(matmul_plain(top_rows, chol_inverse) + identity)
    upper_inverse = upper_inverse_of(upper_f)
    tri_factor = matmul_plain(upper_f, lower_inverse(lower_f).T)
    return (chol_inverse, upper_inverse, tri_factor)

def reflect(product, house, tri_factor):
    prod_rows = matmul_plain(product, tri_factor)
    gram_house = inner_rows(house, product)
    middle = matmul_plain(matmul_plain(tri_factor.T, gram_house), tri_factor)
    return prod_rows - 0.5 * matmul_plain(house, middle)

def reference(matrix):
    order_size = matrix.shape[0]
    band = BAND
    row_ids = jnp.arange(order_size)

    def factor_panel(columns, start_row):
        panel_cols = jnp.where(row_ids[:, None] >= start_row, columns, 0.0)
        picks = (row_ids[:, None] == start_row + jnp.arange(band)[None, :]).astype(jnp.float32)
        gram_sum = inner_rows(panel_cols, panel_cols)
        top_rows = inner_rows(picks, panel_cols)
        chol_inverse, upper_inverse, tri_factor = factor(gram_sum, top_rows)
        house = matmul_plain(matmul_plain(panel_cols, chol_inverse) + picks, upper_inverse)
        return (house, tri_factor)
    house_one, tri_one = factor_panel(matrix[:, :band], band)
    work_one = reflect(matmul_plain(matrix, house_one), house_one, tri_one)
    columns = matrix[:, band:2 * band] - outer_rows(house_one, work_one[band:2 * band]) - outer_rows(work_one, house_one[band:2 * band])
    house_two, tri_two = factor_panel(columns, 2 * band)
    product = matmul_plain(matrix, house_two) - matmul_plain(house_one, inner_rows(work_one, house_two)) - matmul_plain(work_one, inner_rows(house_one, house_two))
    work_two = reflect(product, house_two, tri_two)
    left_side = jnp.concatenate([house_one, work_one, house_two, work_two], 1)
    right_side = jnp.concatenate([work_one, house_one, work_two, house_two], 1)
    return matrix - outer_rows(left_side, right_side)
```

```python
import functools

import jax
import jax.numpy as jnp
from jax import lax
from jax.experimental import pallas as pl
from jax.experimental.pallas import tpu as pltpu
from jax.sharding import PartitionSpec as P

BAND = 128
HIGH = lax.Precision.HIGHEST
VMEM = pltpu.VMEM
MESH = pl.DeviceIdType.MESH


def dot(left, right):
    return jnp.dot(left, right, precision=HIGH, preferred_element_type=jnp.float32)


def mm(left, right, ca=1, cb=0):
    return lax.dot_general(
        left, right, (((ca,), (cb,)), ((), ())), precision=HIGH, preferred_element_type=jnp.float32
    )


def eliminate(x_ref, jordan):
    n = x_ref.shape[0]
    lane = lax.broadcasted_iota(jnp.int32, (1, n), 1)
    rows = lax.broadcasted_iota(jnp.int32, (n, 1), 0)
    rows8 = lax.broadcasted_iota(jnp.int32, (8, 1), 0)

    def block(j, _):
        full = x_ref[...]
        strip = x_ref[pl.ds(pl.multiple_of(8 * j, 8), 8), :]
        for i in range(8):
            row = strip[i : i + 1, :]
            inv = 1.0 / row[:, i : i + 1]
            here = lane == i
            row = jnp.where(here, 1.0, row)

            def update(x, ids):
                col = x[:, i : i + 1] * inv
                if jordan:
                    pivot = ids == i
                    col = jnp.where(pivot, -inv, col)
                    return jnp.where(here | pivot, 0.0, x) - col * row
                below = ids > i
                col = jnp.where(below, col, 0.0)
                return jnp.where(here & below, 0.0, x) - col * row

            full = update(full, rows - 8 * j)
            strip = update(strip, rows8)
        x_ref[...] = pltpu.roll(full, n - 8, 1)
        return 0

    lax.fori_loop(0, n // 8, block, 0)


def piece(ref, k):
    parts, _, n = ref.shape
    rows = BAND // parts
    return ref[:, k * rows : (k + 1) * rows, :].reshape(BAND, n)


def factor_kernel(g_ref, t_ref, cinv_ref, rinv_ref, f_ref, ft_ref, finv_ref, finvt_ref):
    n = BAND
    r = lax.broadcasted_iota(jnp.int32, (n, n), 0)
    c = lax.broadcasted_iota(jnp.int32, (n, n), 1)
    eye = (r == c).astype(jnp.float32)
    cinv_ref[...] = piece(g_ref, 0)
    eliminate(cinv_ref, False)
    x = cinv_ref[...]
    diag = jnp.sum(jnp.where(r == c, x, 0.0), axis=1, keepdims=True)
    scale = 1.0 / jnp.sqrt(diag)
    cinv = jnp.where(r > c, x, eye) * scale
    cinv = jnp.where(r >= c, cinv, 0.0)
    cinv_ref[...] = cinv
    rinv_ref[...] = cinv.T
    f = dot(t_ref[...] if len(t_ref.shape) == 2 else piece(t_ref, 1), rinv_ref[...]) + eye
    f_ref[...] = f
    ft_ref[...] = f.T
    finv_ref[...] = f
    eliminate(finv_ref, True)
    finvt_ref[...] = finv_ref[...].T


def factor(gram, top):
    shape = jax.ShapeDtypeStruct((BAND, BAND), jnp.float32)
    return pl.pallas_call(
        factor_kernel,
        out_shape=(shape,) * 6,
        in_specs=[pl.BlockSpec(memory_space=VMEM)] * 2,
        out_specs=(pl.BlockSpec(memory_space=VMEM),) * 6,
        cost_estimate=pl.CostEstimate(flops=40_000_000, bytes_accessed=400_000_000, transcendentals=0),
        name="factor",
    )(gram, top)


def weights(fac, h, s_top, s_topt, a_ss):
    cinv, rinv, _, _, finv, finvt = fac
    half = dot(cinv, h) + s_top
    j = dot(half, rinv) + dot(cinv, s_topt) + a_ss
    return dot(dot(finv, j), finvt)


def step_one_kernel(
    pos_ref, cinv_ref, rinv_ref, f_ref, ft_ref, finv_ref, finvt_ref, h_ref, ht_ref, g_ref,
    pr_ref, sr_ref, pc_ref, sc_ref,
    left_ref, right_ref, p2r_ref, p2c_ref, e2r_ref, e2c_ref, t2_ref, a33_ref, small_ref,
):
    b = BAND
    n = pr_ref.shape[0]
    always = pos_ref[0] >= 0
    sums = lambda k: h_ref[k * b : (k + 1) * b, :]
    sumst = lambda k: ht_ref[:, k * b : (k + 1) * b]
    a22, a31, a32, a33, a13, a23 = (functools.partial(piece, g_ref, k) for k in range(2, 8))

    @pl.when(always)
    def _():
        fac = tuple(ref[...] for ref in (cinv_ref, rinv_ref, f_ref, ft_ref, finv_ref, finvt_ref))
        small_ref[0, :, :] = weights(fac, sums(0), sums(1), sumst(1), a22())

    @pl.when(always)
    def _():
        small_ref[6, :, :] = dot(a31(), rinv_ref[...])
        small_ref[3, :, :] = dot(cinv_ref[...], a13())

    def work(slot, house, sums, cols):
        @pl.when(always)
        def _():
            rows = dot(dot(sums, rinv_ref[...]) + cols(), finvt_ref[...])
            small_ref[slot, :, :] = rows - 0.5 * dot(house(), small_ref[0])

    def workt(slot, house, sums, cols):
        @pl.when(always)
        def _():
            rows = dot(finv_ref[...], dot(cinv_ref[...], sums) + cols())
            small_ref[slot, :, :] = rows - 0.5 * dot(small_ref[0], house())

    work(5, lambda: small_ref[6], sums(2), a32)
    work(4, lambda: f_ref[...], sums(1), a22)
    workt(1, lambda: ft_ref[...], sumst(1), a22)
    workt(2, lambda: small_ref[3], sumst(2), a23)

    @pl.when(always)
    def _():
        t2_ref[...] = a32() - dot(small_ref[6], small_ref[1]) - dot(small_ref[5], ft_ref[...])
        a33_ref[...] = a33() - dot(small_ref[6], small_ref[2]) - dot(small_ref[5], small_ref[3])

    tile = 2 * b if n % (2 * b) == 0 else b

    def side(start, p_ref, s_ref, out_ref, house_at, work_at, p2_ref, e2_ref):
        @pl.loop(0, n // tile)
        def _(step):
            at = pl.ds(pl.multiple_of(step * tile, tile), tile)
            ids = start * n + step * tile + lax.broadcasted_iota(jnp.int32, (tile, b), 0)
            lane = lax.broadcasted_iota(jnp.int32, (tile, b), 1)
            panel = jnp.where(ids >= b, p_ref[at, 0:b], 0.0)
            house = dot(panel, rinv_ref[...]) + (ids - b == lane).astype(jnp.float32)
            cols = p_ref[at, b : 2 * b]
            wk = dot(dot(s_ref[at, :], rinv_ref[...]) + cols, finvt_ref[...]) - 0.5 * dot(house, small_ref[0])
            out_ref[at, house_at : house_at + b] = house
            out_ref[at, work_at : work_at + b] = wk
            p2 = cols - dot(house, small_ref[1]) - dot(wk, ft_ref[...])
            p2_ref[at, :] = jnp.where(ids >= 2 * b, p2, 0.0)
            e2_ref[at, :] = p_ref[at, 2 * b : 3 * b] - dot(house, small_ref[2]) - dot(wk, small_ref[3])

    side(pos_ref[0], pr_ref, sr_ref, left_ref, 0, b, p2r_ref, e2r_ref)
    side(pos_ref[1], pc_ref, sc_ref, right_ref, b, 0, p2c_ref, e2c_ref)


def step_two_kernel(
    pos_ref, cinv_ref, rinv_ref, f_ref, ft_ref, finv_ref, finvt_ref, h_ref, ht_ref, a33_ref,
    pr_ref, sr_ref, er_ref, pc_ref, sc_ref, ec_ref,
    left_ref, right_ref, z_ref,
):
    b = BAND
    n = pr_ref.shape[0]
    tile = 2 * b if n % (2 * b) == 0 else b

    @pl.when(pos_ref[0] >= 0)
    def _():
        fac = tuple(ref[...] for ref in (cinv_ref, rinv_ref, f_ref, ft_ref, finv_ref, finvt_ref))
        z_ref[...] = weights(fac, h_ref[0:b, :], h_ref[b : 2 * b, :], ht_ref[:, b : 2 * b], a33_ref[...])

    def side(start, p_ref, s_ref, e_ref, out_ref, house_at, work_at):
        @pl.loop(0, n // tile)
        def _(step):
            at = pl.ds(pl.multiple_of(step * tile, tile), tile)
            ids = start * n + step * tile + lax.broadcasted_iota(jnp.int32, (tile, b), 0)
            lane = lax.broadcasted_iota(jnp.int32, (tile, b), 1)
            house = dot(p_ref[at, :], rinv_ref[...]) + (ids - 2 * b == lane).astype(jnp.float32)
            out_ref[at, house_at : house_at + b] = house
            ay = dot(s_ref[at, :], rinv_ref[...]) + e_ref[at, :]
            out_ref[at, work_at : work_at + b] = dot(ay, finvt_ref[...]) - 0.5 * dot(house, z_ref[...])

    side(pos_ref[0], pr_ref, sr_ref, er_ref, left_ref, 0, b)
    side(pos_ref[1], pc_ref, sc_ref, ec_ref, right_ref, b, 0)


def call(body, outs, name, scratch=()):
    def run(pos, *args):
        return pl.pallas_call(
            body,
            out_shape=tuple(jax.ShapeDtypeStruct(s, jnp.float32) for s in outs),
            in_specs=[pl.BlockSpec(memory_space=pltpu.SMEM)] + [pl.BlockSpec(memory_space=VMEM)] * len(args),
            out_specs=(pl.BlockSpec(memory_space=VMEM),) * len(outs),
            scratch_shapes=scratch,
            name=name,
        )(pos, *args)

    return run


def greet(nr, nc):
    r, c = lax.axis_index("row"), lax.axis_index("col")
    barrier = pltpu.get_barrier_semaphore()
    for k in range(1, nc):
        pl.semaphore_signal(barrier, inc=1, device_id=(r, (c + k) % nc), device_id_type=MESH)
    for k in range(1, nr):
        pl.semaphore_signal(barrier, inc=1, device_id=((r + k) % nr, c), device_id_type=MESH)
    pl.semaphore_wait(barrier, nr + nc - 2)
    return r, c


def rows_at(index, size):
    return pl.ds(pl.multiple_of(index * size, 8), size)


def spread_kernel(nr, nc, xr, xc, pr, pc, root_send, root_recv, send, recv):
    r, c = greet(nr, nc)
    sides = (
        (0, nc, c, xr, pr, lambda k: (r, k)),
        (1, nr, r, xc, pc, lambda k: (k, c)),
    )

    def scatter(side, size, src, dst, dev, k):
        return pltpu.make_async_remote_copy(
            src_ref=src.at[pl.ds(k * size, size)],
            dst_ref=dst.at[pl.ds(k * size, size)],
            send_sem=root_send.at[side, k],
            recv_sem=root_recv.at[side],
            device_id=dev(k),
            device_id_type=MESH,
        )

    for side, parts, me, src, dst, dev in sides:
        size = src.shape[0] // parts

        @pl.when(me == 0)
        def _():
            for k in range(1, parts):
                scatter(side, size, src, dst, dev, k).start()
            dst[0:size, :] = src[0:size, :]

    copies = []
    for side, parts, me, src, dst, dev in sides:
        size = src.shape[0] // parts

        @pl.when(me != 0)
        def _():
            scatter(side, size, src, dst, dev, 1).wait_recv()

        for k in range(1, parts):
            copy = pltpu.make_async_remote_copy(
                src_ref=dst.at[rows_at(me, size)],
                dst_ref=dst.at[rows_at(me, size)],
                send_sem=send.at[side, k],
                recv_sem=recv.at[side, k],
                device_id=dev((me + k) % parts),
                device_id_type=MESH,
            )
            copy.start()
            copies.append(copy)
    for copy in copies:
        copy.wait()
    for side, parts, me, src, dst, dev in sides:
        size = src.shape[0] // parts

        @pl.when(me == 0)
        def _():
            for k in range(1, parts):
                scatter(side, size, src, dst, dev, k).wait_send()


def reduce_kernel(
    nr, nc, sr, sc, h, g, out_r, out_c, out_h, out_g,
    part_r, part_c, part_h, part_g, sum_r, sum_c, sum_h, sum_g, cols_h, all_h, send, recv,
):
    r, c = greet(nr, nc)
    size_r, size_c, size_h = sr.shape[0] // nc, sc.shape[0] // nr, h.shape[0] // nc

    def along(axis, phase, source, target):
        parts, me = (nc, c) if axis == "col" else (nr, r)
        copies = []
        for k in range(1, parts):
            to = (me + k) % parts
            copy = pltpu.make_async_remote_copy(
                src_ref=source(to),
                dst_ref=target(k),
                send_sem=send.at[phase, k],
                recv_sem=recv.at[phase, k],
                device_id=(r, to) if axis == "col" else (to, c),
                device_id_type=MESH,
            )
            copy.start()
            copies.append(copy)
        return copies

    def finish(copies):
        for copy in copies:
            copy.wait()

    g_copies = along("row", 0, lambda to: g, lambda k: part_g.at[r])
    h_copies = along("col", 1, lambda to: h.at[rows_at(to, size_h)], lambda k: part_h.at[k])
    r_copies = along("col", 2, lambda to: sr.at[rows_at(to, size_r)], lambda k: part_r.at[k])
    c_copies = along("row", 3, lambda to: sc.at[rows_at(to, size_c)], lambda k: part_c.at[k])
    part_g[r] = g[...]

    def add(parts, count, start):
        value = start
        for k in range(count):
            value = parts[k] if value is None else value + parts[k]
        return value

    finish(g_copies)
    value = add(part_g, nr, None)
    sum_g[...] = value
    out_g[c] = value
    g_copies = along("col", 4, lambda to: sum_g, lambda k: out_g.at[c])

    finish(h_copies)
    value = h[rows_at(c, size_h), :]
    for k in range(1, nc):
        value = value + part_h[k]
    sum_h[...] = value
    cols_h[r] = value
    h_copies = along("row", 5, lambda to: sum_h, lambda k: cols_h.at[r])

    finish(r_copies)
    value = sr[rows_at(c, size_r), :]
    for k in range(1, nc):
        value = value + part_r[k]
    sum_r[...] = value
    out_r[rows_at(c, size_r), :] = value
    r_copies = along("col", 6, lambda to: sum_r, lambda k: out_r.at[rows_at(c, size_r)])

    finish(c_copies)
    value = sc[rows_at(r, size_c), :]
    for k in range(1, nr):
        value = value + part_c[k]
    sum_c[...] = value
    out_c[rows_at(r, size_c), :] = value
    c_copies = along("row", 7, lambda to: sum_c, lambda k: out_c.at[rows_at(r, size_c)])

    finish(h_copies)
    value = add(cols_h, nr, None)
    all_h[...] = value
    out_h[rows_at(c, size_h), :] = value
    h_copies = along("col", 8, lambda to: all_h, lambda k: out_h.at[rows_at(c, size_h)])
    for copies in (g_copies, r_copies, c_copies, h_copies):
        finish(copies)


def spread(nr, nc, xr, xc):
    most = max(nr, nc)
    dma = pltpu.SemaphoreType.DMA
    return pl.pallas_call(
        functools.partial(spread_kernel, nr, nc),
        out_shape=tuple(jax.ShapeDtypeStruct(x.shape, jnp.float32) for x in (xr, xc)),
        in_specs=[pl.BlockSpec(memory_space=VMEM)] * 2,
        out_specs=(pl.BlockSpec(memory_space=VMEM),) * 2,
        scratch_shapes=[dma((2, most)), dma((2,)), dma((2, most)), dma((2, most))],
        compiler_params=pltpu.CompilerParams(collective_id=0, has_side_effects=True),
        name="spread",
    )(xr, xc)


def reduce(nr, nc, sr, sc, h, g, which):
    most = max(nr, nc)
    dma = pltpu.SemaphoreType.DMA
    b = sr.shape[1]
    size_r, size_c, size_h, size_g = sr.shape[0] // nc, sc.shape[0] // nr, h.shape[0] // nc, g.shape[0]
    outs = (sr.shape, sc.shape, h.shape, (nc, size_g, b))
    scratch = [
        (nc, size_r, b), (nr, size_c, b), (nc, size_h, b), (nr, size_g, b),
        (size_r, b), (size_c, b), (size_h, b), (size_g, b), (nr, size_h, b), (size_h, b),
    ]
    return pl.pallas_call(
        functools.partial(reduce_kernel, nr, nc),
        out_shape=tuple(jax.ShapeDtypeStruct(s, jnp.float32) for s in outs),
        in_specs=[pl.BlockSpec(memory_space=VMEM)] * 4,
        out_specs=(pl.BlockSpec(memory_space=VMEM),) * 4,
        scratch_shapes=[VMEM(s, jnp.float32) for s in scratch] + [dma((9, most)), dma((9, most))],
        compiler_params=pltpu.CompilerParams(collective_id=which, has_side_effects=True),
        name=f"reduce_{which}",
    )(sr, sc, h, g)


def shards(nr, nc, matrix):
    n = matrix.shape[0]
    b = BAND
    row, col = lax.axis_index("row"), lax.axis_index("col")
    pos = jnp.stack([row, col]).astype(jnp.int32)
    row_ids = row * n + jnp.arange(n, dtype=jnp.int32)
    col_ids = col * n + jnp.arange(n, dtype=jnp.int32)

    def slices(blocks):
        size = b // nc
        picked = lax.dynamic_slice_in_dim(jnp.stack(blocks), col * size, size, 1)
        return picked.reshape(len(blocks) * size, b)

    def products(current, rows, cols, first, last):
        sr = mm(current, cols)
        sc = mm(current, rows, 0, 0)
        head = jnp.where(row == 0, sr[first * b : last * b], 0.0)
        return sr, sc, jnp.concatenate([mm(rows, sr, 0, 0), head], 0)

    pr, pc = spread(nr, nc, matrix[:, : 3 * b], matrix[: 3 * b, :].T)
    p1r = jnp.where(row_ids[:, None] >= b, pr[:, :b], 0.0)
    p1c = jnp.where(col_ids[:, None] >= b, pc[:, :b], 0.0)
    corner = jnp.where(row == 0, pr[: 3 * b], 0.0)
    where = ((1, 0), (1, 1), (2, 0), (2, 1), (2, 2), (0, 2), (1, 2))
    tops = [corner[i * b : (i + 1) * b, j * b : (j + 1) * b] for i, j in where]
    g = slices([mm(p1r, p1r, 0, 0), *tops])
    sr, sc, h, g = reduce(nr, nc, *products(matrix, p1r, p1c, 1, 3), g, 1)
    fac = factor(g, g)
    one = call(
        step_one_kernel,
        [(n, 2 * b), (n, 2 * b), (n, b), (n, b), (n, b), (n, b), (b, b), (b, b)],
        "step_one",
        [VMEM((7, b, b), jnp.float32)],
    )
    left, right, p2r, p2c, e2r, e2c, t2, a33 = one(pos, *fac, h, h.T, g, pr, sr, pc, sc)
    updated = matrix - mm(left, right, 1, 1)
    sr2, sc2, h2, g2 = reduce(nr, nc, *products(updated, p2r, p2c, 2, 3), slices([mm(p2r, p2r, 0, 0)]), 2)
    fac2 = factor(g2, t2)
    two = call(step_two_kernel, [(n, 2 * b), (n, 2 * b)], "step_two", [VMEM((b, b), jnp.float32)])
    left2, right2 = two(pos, *fac2, h2, h2.T, a33, p2r, sr2, e2r, p2c, sc2, e2c)
    return updated - mm(left2, right2, 1, 1)


def solution(mesh):
    spec = P("row", "col")
    body = functools.partial(shards, mesh.shape["row"], mesh.shape["col"])
    return jax.shard_map(body, mesh=mesh, in_specs=(spec,), out_specs=spec, check_vma=False)
```

```python
import functools

import jax
import jax.numpy as jnp
from jax import lax
from jax.experimental import pallas as pl
from jax.experimental.pallas import tpu as pltpu
from jax.sharding import PartitionSpec as P

BAND = 128
HIGH = lax.Precision.HIGHEST
VMEM = pltpu.VMEM
MESH = pl.DeviceIdType.MESH


def dot(left, right):
    return jnp.dot(left, right, precision=HIGH, preferred_element_type=jnp.float32)


def mm(left, right, ca=1, cb=0):
    return lax.dot_general(
        left, right, (((ca,), (cb,)), ((), ())), precision=HIGH, preferred_element_type=jnp.float32
    )


def eliminate(x_ref, jordan):
    n = x_ref.shape[0]
    lane = lax.broadcasted_iota(jnp.int32, (1, n), 1)
    rows = lax.broadcasted_iota(jnp.int32, (n, 1), 0)
    rows8 = lax.broadcasted_iota(jnp.int32, (8, 1), 0)

    def block(j, _):
        full = x_ref[...]
        strip = x_ref[pl.ds(pl.multiple_of(8 * j, 8), 8), :]
        for i in range(8):
            row = strip[i : i + 1, :]
            inv = 1.0 / row[:, i : i + 1]
            here = lane == i
            row = jnp.where(here, 1.0, row)

            def update(x, ids):
                col = x[:, i : i + 1] * inv
                if jordan:
                    pivot = ids == i
                    col = jnp.where(pivot, -inv, col)
                    return jnp.where(here | pivot, 0.0, x) - col * row
                below = ids > i
                col = jnp.where(below, col, 0.0)
                return jnp.where(here & below, 0.0, x) - col * row

            full = update(full, rows - 8 * j)
            strip = update(strip, rows8)
        x_ref[...] = pltpu.roll(full, n - 8, 1)
        return 0

    lax.fori_loop(0, n // 8, block, 0)


def piece(ref, k):
    parts, _, n = ref.shape
    rows = BAND // parts
    return ref[:, k * rows : (k + 1) * rows, :].reshape(BAND, n)


def whole(ref):
    parts, rows, n = ref.shape
    return ref[...].reshape(parts * rows, n)


def invert_chol(gram, cinv_ref, rinv_ref):
    n = BAND
    r = lax.broadcasted_iota(jnp.int32, (n, n), 0)
    c = lax.broadcasted_iota(jnp.int32, (n, n), 1)
    cinv_ref[...] = gram
    eliminate(cinv_ref, False)
    x = cinv_ref[...]
    diag = jnp.sum(jnp.where(r == c, x, 0.0), axis=1, keepdims=True)
    cinv = jnp.where(r > c, x, (r == c).astype(jnp.float32)) / jnp.sqrt(diag)
    cinv_ref[...] = cinv
    rinv_ref[...] = cinv.T


def invert_top(top, rinv_ref, f_ref, ft_ref, finv_ref, finvt_ref):
    n = BAND
    r = lax.broadcasted_iota(jnp.int32, (n, n), 0)
    c = lax.broadcasted_iota(jnp.int32, (n, n), 1)
    f = dot(top, rinv_ref[...]) + (r == c).astype(jnp.float32)
    f_ref[...] = f
    ft_ref[...] = f.T
    finv_ref[...] = f
    eliminate(finv_ref, True)
    finvt_ref[...] = finv_ref[...].T


def weights(fac, h, s_top, s_topt, a_ss):
    cinv, rinv, _, _, finv, finvt = fac
    half = dot(cinv, h) + s_top
    j = dot(half, rinv) + dot(cinv, s_topt) + a_ss
    return dot(dot(finv, j), finvt)


def step_one_kernel(
    pos_ref, cinv_ref, rinv_ref, f_ref, ft_ref, finv_ref, finvt_ref, h_ref, ht_ref, g_ref,
    pr_ref, sr_ref, er_ref, pc_ref, sc_ref, ec_ref,
    left_ref, right_ref, p2r_ref, p2c_ref, t2_ref, a33_ref, small_ref,
):
    b = BAND
    n = pr_ref.shape[0]
    always = pos_ref[0] >= 0
    sums = lambda k: h_ref[k * b : (k + 1) * b, :]
    sumst = lambda k: ht_ref[:, k * b : (k + 1) * b]
    a22, a31, a32, a33, a13, a23 = (functools.partial(piece, g_ref, k) for k in range(1, 7))

    @pl.when(always)
    def _():
        fac = tuple(ref[...] for ref in (cinv_ref, rinv_ref, f_ref, ft_ref, finv_ref, finvt_ref))
        small_ref[0, :, :] = weights(fac, sums(0), sums(1), sumst(1), a22())

    @pl.when(always)
    def _():
        small_ref[6, :, :] = dot(a31(), rinv_ref[...])
        small_ref[3, :, :] = dot(cinv_ref[...], a13())

    def work(slot, house, sums, cols):
        @pl.when(always)
        def _():
            rows = dot(dot(sums, rinv_ref[...]) + cols(), finvt_ref[...])
            small_ref[slot, :, :] = rows - 0.5 * dot(house(), small_ref[0])

    def workt(slot, house, sums, cols):
        @pl.when(always)
        def _():
            rows = dot(finv_ref[...], dot(cinv_ref[...], sums) + cols())
            small_ref[slot, :, :] = rows - 0.5 * dot(small_ref[0], house())

    work(5, lambda: small_ref[6], sums(2), a32)
    work(4, lambda: f_ref[...], sums(1), a22)
    workt(1, lambda: ft_ref[...], sumst(1), a22)
    workt(2, lambda: small_ref[3], sumst(2), a23)

    @pl.when(always)
    def _():
        t2_ref[...] = a32() - dot(small_ref[6], small_ref[1]) - dot(small_ref[5], ft_ref[...])
        a33_ref[...] = a33() - dot(small_ref[6], small_ref[2]) - dot(small_ref[5], small_ref[3])

    tile = 2 * b if n % (2 * b) == 0 else b

    def side(start, p_ref, s_ref, e_ref, out_ref, house_at, work_at, p2_ref):
        @pl.loop(0, n // tile)
        def _(step):
            at = pl.ds(pl.multiple_of(step * tile, tile), tile)
            ids = start * n + step * tile + lax.broadcasted_iota(jnp.int32, (tile, b), 0)
            lane = lax.broadcasted_iota(jnp.int32, (tile, b), 1)
            house = dot(p_ref[at, :], rinv_ref[...]) + (ids - b == lane).astype(jnp.float32)
            cols = e_ref[at, :]
            wk = dot(dot(s_ref[at, :], rinv_ref[...]) + cols, finvt_ref[...]) - 0.5 * dot(house, small_ref[0])
            out_ref[at, house_at : house_at + b] = house
            out_ref[at, work_at : work_at + b] = wk
            p2 = cols - dot(house, small_ref[1]) - dot(wk, ft_ref[...])
            p2_ref[at, :] = jnp.where(ids >= 2 * b, p2, 0.0)

    side(pos_ref[0], pr_ref, sr_ref, er_ref, left_ref, 0, b, p2r_ref)
    side(pos_ref[1], pc_ref, sc_ref, ec_ref, right_ref, b, 0, p2c_ref)


def step_two_kernel(
    pos_ref, cinv_ref, rinv_ref, f_ref, ft_ref, finv_ref, finvt_ref, h_ref, ht_ref, a33_ref,
    pr_ref, sr_ref, er_ref, pc_ref, sc_ref, ec_ref,
    left_ref, right_ref, z_ref,
):
    b = BAND
    n = pr_ref.shape[0]
    tile = 2 * b if n % (2 * b) == 0 else b

    @pl.when(pos_ref[0] >= 0)
    def _():
        fac = tuple(ref[...] for ref in (cinv_ref, rinv_ref, f_ref, ft_ref, finv_ref, finvt_ref))
        z_ref[...] = weights(fac, h_ref[0:b, :], h_ref[b : 2 * b, :], ht_ref[:, b : 2 * b], a33_ref[...])

    def side(start, p_ref, s_ref, e_ref, out_ref, house_at, work_at):
        @pl.loop(0, n // tile)
        def _(step):
            at = pl.ds(pl.multiple_of(step * tile, tile), tile)
            ids = start * n + step * tile + lax.broadcasted_iota(jnp.int32, (tile, b), 0)
            lane = lax.broadcasted_iota(jnp.int32, (tile, b), 1)
            house = dot(p_ref[at, :], rinv_ref[...]) + (ids - 2 * b == lane).astype(jnp.float32)
            out_ref[at, house_at : house_at + b] = house
            ay = dot(s_ref[at, :], rinv_ref[...]) + e_ref[at, :]
            out_ref[at, work_at : work_at + b] = dot(ay, finvt_ref[...]) - 0.5 * dot(house, z_ref[...])

    side(pos_ref[0], pr_ref, sr_ref, er_ref, left_ref, 0, b)
    side(pos_ref[1], pc_ref, sc_ref, ec_ref, right_ref, b, 0)


def call(body, outs, name, scratch=()):
    def run(pos, *args):
        return pl.pallas_call(
            body,
            out_shape=tuple(jax.ShapeDtypeStruct(s, jnp.float32) for s in outs),
            in_specs=[pl.BlockSpec(memory_space=pltpu.SMEM)] + [pl.BlockSpec(memory_space=VMEM)] * len(args),
            out_specs=(pl.BlockSpec(memory_space=VMEM),) * len(outs),
            scratch_shapes=scratch,
            name=name,
        )(pos, *args)

    return run


def greet(nr, nc):
    r, c = lax.axis_index("row"), lax.axis_index("col")
    barrier = pltpu.get_barrier_semaphore()
    for k in range(1, nc):
        pl.semaphore_signal(barrier, inc=1, device_id=(r, (c + k) % nc), device_id_type=MESH)
    for k in range(1, nr):
        pl.semaphore_signal(barrier, inc=1, device_id=((r + k) % nr, c), device_id_type=MESH)
    pl.semaphore_wait(barrier, nr + nc - 2)
    return r, c


def rows_at(index, size):
    return pl.ds(pl.multiple_of(index * size, 8), size)


class Spread:
    def __init__(self, axis, parts, me, other, dst, sems):
        self.axis, self.parts, self.me, self.other, self.dst = axis, parts, me, other, dst
        self.root_send, self.root_recv, self.send, self.recv = sems
        self.size = dst.shape[0] // parts

    def device(self, k):
        return (self.other, k) if self.axis == "col" else (k, self.other)

    def copy(self, k, src):
        rows = pl.ds(k * self.size, self.size)
        return pltpu.make_async_remote_copy(
            src_ref=src(rows),
            dst_ref=self.dst.at[rows],
            send_sem=self.root_send.at[k],
            recv_sem=self.root_recv,
            device_id=self.device(k),
            device_id_type=MESH,
        )

    def scatter(self, src):
        @pl.when(self.me == 0)
        def _():
            for k in range(1, self.parts):
                self.copy(k, src).start()
            rows = pl.ds(0, self.size)
            self.dst[rows, :] = src(rows)[...]

    def gather(self, src):
        @pl.when(self.me != 0)
        def _():
            self.copy(1, src).wait_recv()

        self.copies = []
        for k in range(1, self.parts):
            rows = rows_at(self.me, self.size)
            copy = pltpu.make_async_remote_copy(
                src_ref=self.dst.at[rows],
                dst_ref=self.dst.at[rows],
                send_sem=self.send.at[k],
                recv_sem=self.recv.at[k],
                device_id=self.device((self.me + k) % self.parts),
                device_id_type=MESH,
            )
            copy.start()
            self.copies.append(copy)

    def finish(self, src):
        for copy in self.copies:
            copy.wait()

        @pl.when(self.me == 0)
        def _():
            for k in range(1, self.parts):
                self.copy(k, src).wait_send()


def spread_sems(parts):
    dma = pltpu.SemaphoreType.DMA
    return [dma((parts,)), dma, dma((parts,)), dma((parts,))]


def spread_kernel(nr, nc, xr, xc, t, pr, pc, ts, *sems):
    rows_sems, cols_sems, (send, recv, down_send, down_recv) = sems[:4], sems[4:8], sems[8:]
    r, c = greet(nr, nc)
    rows = Spread("col", nc, c, r, pr, rows_sems)
    cols = Spread("row", nr, r, c, pc, cols_sems)
    rows.scatter(lambda at: xr.at[at])
    cols.scatter(lambda at: xc.at[at])

    def slice_to(k):
        return pltpu.make_async_remote_copy(
            src_ref=t.at[k], dst_ref=ts, send_sem=send.at[k], recv_sem=recv, device_id=(r, k), device_id_type=MESH
        )

    def down(k):
        return pltpu.make_async_remote_copy(
            src_ref=ts, dst_ref=ts, send_sem=down_send.at[k], recv_sem=down_recv, device_id=(k, c), device_id_type=MESH
        )

    @pl.when((r == 0) & (c == 0))
    def _():
        for k in range(1, nc):
            slice_to(k).start()
        ts[...] = t[0]

    rows.gather(lambda at: xr.at[at])
    cols.gather(lambda at: xc.at[at])

    @pl.when((r == 0) & (c != 0))
    def _():
        slice_to(1).wait_recv()

    @pl.when(r == 0)
    def _():
        for k in range(1, nr):
            down(k).start()

    @pl.when(r != 0)
    def _():
        down(1).wait_recv()

    rows.finish(lambda at: xr.at[at])
    cols.finish(lambda at: xc.at[at])

    @pl.when(r == 0)
    def _():
        for k in range(1, nr):
            down(k).wait_send()

    @pl.when((r == 0) & (c == 0))
    def _():
        for k in range(1, nc):
            slice_to(k).wait_send()


def middle_kernel(
    nr, nc, first, count, gather, a, pr, pc, xc, t, cinv, rinv, f, ft, finv, finvt, out_r, out_c, out_h, er, ec, *rest
):
    out_t, rest = (rest[0], rest[1:]) if gather else (None, rest)
    sr, sc, h, gram, part_r, part_c, part_h, part_g, sum_r, sum_c, sum_h, sum_g, all_g, cols_h, all_h = rest[:15]
    send, recv, *sems = rest[15:]
    b = BAND
    n = a.shape[0]
    size_r, size_c, size_h, size_g = n // nc, n // nr, h.shape[0] // nc, b // nc
    r, c = greet(nr, nc)
    always = r >= 0

    def along(axis, phase, source, target):
        parts, me = (nc, c) if axis == "col" else (nr, r)
        copies = []
        for k in range(1, parts):
            to = (me + k) % parts
            copy = pltpu.make_async_remote_copy(
                src_ref=source(to),
                dst_ref=target(k),
                send_sem=send.at[phase, k],
                recv_sem=recv.at[phase, k],
                device_id=(r, to) if axis == "col" else (to, c),
                device_id_type=MESH,
            )
            copy.start()
            copies.append(copy)
        return copies

    def finish(copies):
        for copy in copies:
            copy.wait()

    def block(body):
        pl.when(always)(body)

    @block
    def _():
        gram[...] = mm(pr[...], pr[...], 0, 0)
        part_g[r] = gram[rows_at(c, size_g), :]

    g_copies = along("row", 0, lambda to: gram.at[rows_at(c, size_g)], lambda k: part_g.at[r])
    t_copies = []
    if gather:
        t_copies = along("col", 1, lambda to: t, lambda k: out_t.at[c])
        out_t[c] = t[...]
    rows = Spread("col", nc, c, r, er, sems[:4])
    cols = Spread("row", nr, r, c, ec, sems[4:])
    rows_src = lambda at: a.at[at, first * b : (first + 1) * b]
    cols_src = lambda at: xc.at[at]
    rows.scatter(rows_src)
    cols.scatter(cols_src)

    tile = 2 * b if n % (2 * b) == 0 else b

    @pl.loop(0, n // tile)
    def _(step):
        at = pl.ds(pl.multiple_of(step * tile, tile), tile)
        sr[at, :] = dot(a[at, :], pc[...])

    r_copies = along("col", 2, lambda to: sr.at[rows_at(to, size_r)], lambda k: part_r.at[k])

    finish(g_copies)
    value = part_g[0]
    for k in range(1, nr):
        value = value + part_g[k]
    sum_g[...] = value
    all_g[c] = value
    g_copies = along("col", 3, lambda to: sum_g, lambda k: all_g.at[c])

    @block
    def _():
        h[0:b, :] = mm(pr[...], sr[...], 0, 0)
        h[b : (1 + count) * b, :] = jnp.where(r == 0, sr[first * b : (first + count) * b, :], 0.0)

    h_copies = along("col", 4, lambda to: h.at[rows_at(to, size_h)], lambda k: part_h.at[k])

    @pl.loop(0, n // tile)
    def _(step):
        at = pl.ds(pl.multiple_of(step * tile, tile), tile)
        sc[at, :] = mm(a[:, at], pr[...], 0, 0)

    c_copies = along("row", 5, lambda to: sc.at[rows_at(to, size_c)], lambda k: part_c.at[k])
    rows.gather(rows_src)
    cols.gather(cols_src)
    finish(g_copies)

    @block
    def _():
        invert_chol(whole(all_g), cinv, rinv)

    finish(h_copies)
    value = h[rows_at(c, size_h), :]
    for k in range(1, nc):
        value = value + part_h[k]
    sum_h[...] = value
    cols_h[r] = value
    h_copies = along("row", 6, lambda to: sum_h, lambda k: cols_h.at[r])

    finish(r_copies)
    value = sr[rows_at(c, size_r), :]
    for k in range(1, nc):
        value = value + part_r[k]
    sum_r[...] = value
    out_r[rows_at(c, size_r), :] = value
    r_copies = along("col", 7, lambda to: sum_r, lambda k: out_r.at[rows_at(c, size_r)])

    finish(c_copies)
    value = sc[rows_at(r, size_c), :]
    for k in range(1, nr):
        value = value + part_c[k]
    sum_c[...] = value
    out_c[rows_at(r, size_c), :] = value
    c_copies = along("row", 8, lambda to: sum_c, lambda k: out_c.at[rows_at(r, size_c)])
    finish(t_copies)

    @block
    def _():
        invert_top(piece(out_t, 0) if gather else t[...], rinv, f, ft, finv, finvt)

    finish(h_copies)
    value = cols_h[0]
    for k in range(1, nr):
        value = value + cols_h[k]
    all_h[...] = value
    out_h[rows_at(c, size_h), :] = value
    h_copies = along("col", 9, lambda to: all_h, lambda k: out_h.at[rows_at(c, size_h)])
    for copies in (r_copies, c_copies, h_copies):
        finish(copies)
    rows.finish(rows_src)
    cols.finish(cols_src)


def spread(nr, nc, xr, xc, t):
    dma = pltpu.SemaphoreType.DMA
    return pl.pallas_call(
        functools.partial(spread_kernel, nr, nc),
        out_shape=tuple(jax.ShapeDtypeStruct(s, jnp.float32) for s in (xr.shape, xc.shape, t.shape[1:])),
        in_specs=[pl.BlockSpec(memory_space=VMEM)] * 3,
        out_specs=(pl.BlockSpec(memory_space=VMEM),) * 3,
        scratch_shapes=[*spread_sems(nc), *spread_sems(nr), dma((nc,)), dma, dma((nr,)), dma],
        compiler_params=pltpu.CompilerParams(collective_id=0, has_side_effects=True),
        name="spread",
    )(xr, xc, t)


def middle(nr, nc, first, count, gather, a, pr, pc, xc, t):
    most = max(nr, nc)
    dma = pltpu.SemaphoreType.DMA
    b = BAND
    n = a.shape[0]
    heads = (1 + count) * b
    size_r, size_c, size_h, size_g = n // nc, n // nr, heads // nc, b // nc
    outs = [(b, b)] * 6 + [(n, b), (n, b), (heads, b), (n, b), (n, b)]
    if gather:
        outs.append((nc, *t.shape))
    scratch = [
        (n, b), (n, b), (heads, b), (b, b),
        (nc, size_r, b), (nr, size_c, b), (nc, size_h, b), (nr, size_g, b),
        (size_r, b), (size_c, b), (size_h, b), (size_g, b), (nc, size_g, b), (nr, size_h, b), (size_h, b),
    ]
    return pl.pallas_call(
        functools.partial(middle_kernel, nr, nc, first, count, gather),
        out_shape=tuple(jax.ShapeDtypeStruct(s, jnp.float32) for s in outs),
        in_specs=[pl.BlockSpec(memory_space=VMEM)] * 5,
        out_specs=(pl.BlockSpec(memory_space=VMEM),) * len(outs),
        scratch_shapes=[
            *(VMEM(s, jnp.float32) for s in scratch),
            dma((10, most)), dma((10, most)), *spread_sems(nc), *spread_sems(nr),
        ],
        compiler_params=pltpu.CompilerParams(collective_id=first, has_side_effects=True),
        name=f"middle_{first}",
    )(a, pr, pc, xc, t)


def shards(nr, nc, matrix):
    n = matrix.shape[0]
    b = BAND
    row, col = lax.axis_index("row"), lax.axis_index("col")
    pos = jnp.stack([row, col]).astype(jnp.int32)
    row_ids = row * n + jnp.arange(n, dtype=jnp.int32)
    col_ids = col * n + jnp.arange(n, dtype=jnp.int32)

    where = ((1, 0), (1, 1), (2, 0), (2, 1), (2, 2), (0, 2), (1, 2))
    tops = jnp.stack([matrix[i * b : (i + 1) * b, j * b : (j + 1) * b] for i, j in where])
    tops = tops.reshape(len(where), nc, b // nc, b).transpose(1, 0, 2, 3).reshape(nc, -1, b)
    p1r, p1c, t = spread(
        nr,
        nc,
        jnp.where(row_ids[:, None] >= b, matrix[:, :b], 0.0),
        jnp.where(col_ids[:, None] >= b, matrix[:b].T, 0.0),
        tops,
    )
    *fac, sr, sc, h, er, ec, t = middle(nr, nc, 1, 2, True, matrix, p1r, p1c, matrix[b : 2 * b].T, t)
    one = call(
        step_one_kernel,
        [(n, 2 * b), (n, 2 * b), (n, b), (n, b), (b, b), (b, b)],
        "step_one",
        [VMEM((7, b, b), jnp.float32)],
    )
    left, right, p2r, p2c, t2, a33 = one(pos, *fac, h, h.T, t, p1r, sr, er, p1c, sc, ec)
    updated = matrix - mm(left, right, 1, 1)
    *fac, sr, sc, h, er, ec = middle(nr, nc, 2, 1, False, updated, p2r, p2c, updated[2 * b : 3 * b].T, t2)
    two = call(step_two_kernel, [(n, 2 * b), (n, 2 * b)], "step_two", [VMEM((b, b), jnp.float32)])
    left, right = two(pos, *fac, h, h.T, a33, p2r, sr, er, p2c, sc, ec)
    return updated - mm(left, right, 1, 1)


def solution(mesh):
    spec = P("row", "col")
    body = functools.partial(shards, mesh.shape["row"], mesh.shape["col"])
    return jax.shard_map(body, mesh=mesh, in_specs=(spec,), out_specs=spec, check_vma=False)
```

```python
import functools

import jax
import jax.numpy as jnp
from jax import lax
from jax.experimental import pallas as pl
from jax.experimental.pallas import tpu as pltpu
from jax.sharding import PartitionSpec as P

BAND = 128
HIGH = lax.Precision.HIGHEST
VMEM = pltpu.VMEM
MESH = pl.DeviceIdType.MESH


def dot(left, right):
    return jnp.dot(left, right, precision=HIGH, preferred_element_type=jnp.float32)


def mm(left, right, ca=1, cb=0):
    return lax.dot_general(
        left, right, (((ca,), (cb,)), ((), ())), precision=HIGH, preferred_element_type=jnp.float32
    )


def eliminate(x_ref, jordan):
    n = x_ref.shape[0]
    lane = lax.broadcasted_iota(jnp.int32, (1, n), 1)
    rows = lax.broadcasted_iota(jnp.int32, (n, 1), 0)
    rows8 = lax.broadcasted_iota(jnp.int32, (8, n), 0)
    lane8 = lax.broadcasted_iota(jnp.int32, (8, n), 1)

    def block(j, _):
        at = pl.ds(pl.multiple_of(8 * j, 8), 8)
        full = x_ref[...]
        strip = x_ref[at, :]
        cols = [jnp.broadcast_to(strip[:, i : i + 1], (8, n)) for i in range(8)]
        kept = strip
        for i in range(8):
            if not jordan:
                kept = jnp.where(rows8 == i, strip, kept)
            inv = 1.0 / jnp.broadcast_to(cols[i][i : i + 1, :], (8, n))
            mult = jnp.where(rows8 == i, -inv, cols[i] * inv)
            for k in range(i + 1, 8):
                cols[k] = jnp.where(rows8 == i, 0.0, cols[k]) - mult * cols[k][i : i + 1, :]
            row = jnp.where(lane == i, 1.0, strip[i : i + 1, :])
            strip = jnp.where((rows8 == i) | (lane8 == i), 0.0, strip) - mult * row
        ids = rows - 8 * j
        out = jnp.where(lane < 8, 0.0, full)
        for i in range(8):
            out = out - full[:, i : i + 1] * strip[i : i + 1, :]
        if jordan:
            x_ref[...] = pltpu.roll(out, n - 8, 1)
            x_ref[at, :] = pltpu.roll(strip, n - 8, 1)
        else:
            x_ref[...] = pltpu.roll(jnp.where(ids >= 8, out, full), n - 8, 1)
            x_ref[at, :] = pltpu.roll(kept, n - 8, 1)
        return 0

    lax.fori_loop(0, n // 8, block, 0)


def piece(ref, k):
    parts, _, n = ref.shape
    rows = BAND // parts
    return ref[:, k * rows : (k + 1) * rows, :].reshape(BAND, n)


def whole(ref):
    parts, rows, n = ref.shape
    return ref[...].reshape(parts * rows, n)


def invert_chol(gram, cinv_ref, rinv_ref):
    n = BAND
    r = lax.broadcasted_iota(jnp.int32, (n, n), 0)
    c = lax.broadcasted_iota(jnp.int32, (n, n), 1)
    cinv_ref[...] = gram
    eliminate(cinv_ref, False)
    x = cinv_ref[...]
    diag = jnp.sum(jnp.where(r == c, x, 0.0), axis=1, keepdims=True)
    cinv = jnp.where(r > c, x, (r == c).astype(jnp.float32)) / jnp.sqrt(diag)
    cinv_ref[...] = cinv
    rinv_ref[...] = cinv.T


def invert_top(top, rinv_ref, f_ref, ft_ref, finv_ref, finvt_ref):
    n = BAND
    r = lax.broadcasted_iota(jnp.int32, (n, n), 0)
    c = lax.broadcasted_iota(jnp.int32, (n, n), 1)
    f = dot(top, rinv_ref[...]) + (r == c).astype(jnp.float32)
    f_ref[...] = f
    ft_ref[...] = f.T
    finv_ref[...] = f
    eliminate(finv_ref, True)
    finvt_ref[...] = finv_ref[...].T


def weights(fac, h, s_top, s_topt, a_ss):
    cinv, rinv, _, _, finv, finvt = fac
    half = dot(cinv, h) + s_top
    j = dot(half, rinv) + dot(cinv, s_topt) + a_ss
    return dot(dot(finv, j), finvt)


def step_one_kernel(
    pos_ref, cinv_ref, rinv_ref, f_ref, ft_ref, finv_ref, finvt_ref, h_ref, g_ref,
    pr_ref, sr_ref, er_ref, pc_ref, sc_ref, ec_ref, a_ref,
    updated_ref, p2r_ref, p2c_ref, t2_ref, a33_ref, left_ref, right_ref, ht_ref, small_ref,
):
    b = BAND
    n = pr_ref.shape[0]
    always = pos_ref[0] >= 0
    sums = lambda k: h_ref[k * b : (k + 1) * b, :]
    sumst = lambda k: ht_ref[:, k * b : (k + 1) * b]

    @pl.when(always)
    def _():
        for k in range(3):
            ht_ref[:, k * b : (k + 1) * b] = h_ref[k * b : (k + 1) * b, :].T

    a22, a31, a32, a33, a13, a23 = (functools.partial(piece, g_ref, k) for k in range(1, 7))

    @pl.when(always)
    def _():
        fac = tuple(ref[...] for ref in (cinv_ref, rinv_ref, f_ref, ft_ref, finv_ref, finvt_ref))
        small_ref[0, :, :] = weights(fac, sums(0), sums(1), sumst(1), a22())

    @pl.when(always)
    def _():
        small_ref[6, :, :] = dot(a31(), rinv_ref[...])
        small_ref[3, :, :] = dot(cinv_ref[...], a13())

    def work(slot, house, sums, cols):
        @pl.when(always)
        def _():
            rows = dot(dot(sums, rinv_ref[...]) + cols(), finvt_ref[...])
            small_ref[slot, :, :] = rows - 0.5 * dot(house(), small_ref[0])

    def workt(slot, house, sums, cols):
        @pl.when(always)
        def _():
            rows = dot(finv_ref[...], dot(cinv_ref[...], sums) + cols())
            small_ref[slot, :, :] = rows - 0.5 * dot(small_ref[0], house())

    work(5, lambda: small_ref[6], sums(2), a32)
    work(4, lambda: f_ref[...], sums(1), a22)
    workt(1, lambda: ft_ref[...], sumst(1), a22)
    workt(2, lambda: small_ref[3], sumst(2), a23)

    @pl.when(always)
    def _():
        t2_ref[...] = a32() - dot(small_ref[6], small_ref[1]) - dot(small_ref[5], ft_ref[...])
        a33_ref[...] = a33() - dot(small_ref[6], small_ref[2]) - dot(small_ref[5], small_ref[3])

    tile = 2 * b if n % (2 * b) == 0 else b

    def side(start, p_ref, s_ref, e_ref, out_ref, house_at, work_at, p2_ref):
        @pl.loop(0, n // tile)
        def _(step):
            at = pl.ds(pl.multiple_of(step * tile, tile), tile)
            ids = start * n + step * tile + lax.broadcasted_iota(jnp.int32, (tile, b), 0)
            lane = lax.broadcasted_iota(jnp.int32, (tile, b), 1)
            house = dot(p_ref[at, :], rinv_ref[...]) + (ids - b == lane).astype(jnp.float32)
            cols = e_ref[at, :]
            wk = dot(dot(s_ref[at, :], rinv_ref[...]) + cols, finvt_ref[...]) - 0.5 * dot(house, small_ref[0])
            out_ref[at, house_at : house_at + b] = house
            out_ref[at, work_at : work_at + b] = wk
            p2 = cols - dot(house, small_ref[1]) - dot(wk, ft_ref[...])
            p2_ref[at, :] = jnp.where(ids >= 2 * b, p2, 0.0)

    side(pos_ref[0], pr_ref, sr_ref, er_ref, left_ref, 0, b, p2r_ref)
    side(pos_ref[1], pc_ref, sc_ref, ec_ref, right_ref, b, 0, p2c_ref)

    @pl.loop(0, n // tile)
    def _(step):
        at = pl.ds(pl.multiple_of(step * tile, tile), tile)
        updated_ref[at, :] = a_ref[at, :] - mm(left_ref[at, :], right_ref[...], 1, 1)


def step_two_kernel(
    pos_ref, cinv_ref, rinv_ref, f_ref, ft_ref, finv_ref, finvt_ref, h_ref, a33_ref,
    pr_ref, sr_ref, er_ref, pc_ref, sc_ref, ec_ref, a_ref,
    out_ref, left_ref, right_ref, ht_ref, z_ref, result_ref, sem,
):
    b = BAND
    n = pr_ref.shape[0]
    tile = 2 * b if n % (2 * b) == 0 else b

    @pl.when(pos_ref[0] >= 0)
    def _():
        ht_ref[...] = h_ref[b : 2 * b, :].T

    @pl.when(pos_ref[0] >= 0)
    def _():
        fac = tuple(ref[...] for ref in (cinv_ref, rinv_ref, f_ref, ft_ref, finv_ref, finvt_ref))
        z_ref[...] = weights(fac, h_ref[0:b, :], h_ref[b : 2 * b, :], ht_ref[...], a33_ref[...])

    def side(start, p_ref, s_ref, e_ref, out_ref, house_at, work_at):
        @pl.loop(0, n // tile)
        def _(step):
            at = pl.ds(pl.multiple_of(step * tile, tile), tile)
            ids = start * n + step * tile + lax.broadcasted_iota(jnp.int32, (tile, b), 0)
            lane = lax.broadcasted_iota(jnp.int32, (tile, b), 1)
            house = dot(p_ref[at, :], rinv_ref[...]) + (ids - 2 * b == lane).astype(jnp.float32)
            out_ref[at, house_at : house_at + b] = house
            ay = dot(s_ref[at, :], rinv_ref[...]) + e_ref[at, :]
            out_ref[at, work_at : work_at + b] = dot(ay, finvt_ref[...]) - 0.5 * dot(house, z_ref[...])

    side(pos_ref[0], pr_ref, sr_ref, er_ref, left_ref, 0, b)
    side(pos_ref[1], pc_ref, sc_ref, ec_ref, right_ref, b, 0)

    def store(step):
        at = pl.ds(pl.multiple_of(step * tile, tile), tile)
        return pltpu.make_async_copy(result_ref.at[at], out_ref.at[at], sem.at[step])

    @pl.loop(0, n // tile)
    def _(step):
        at = pl.ds(pl.multiple_of(step * tile, tile), tile)
        result_ref[at, :] = a_ref[at, :] - mm(left_ref[at, :], right_ref[...], 1, 1)
        store(step).start()

    @pl.loop(0, n // tile)
    def _(step):
        store(step).wait()


def call(body, outs, name, scratch, space=VMEM):
    def run(pos, *args):
        return pl.pallas_call(
            body,
            out_shape=tuple(jax.ShapeDtypeStruct(s, jnp.float32) for s in outs),
            in_specs=[pl.BlockSpec(memory_space=pltpu.SMEM)] + [pl.BlockSpec(memory_space=VMEM)] * len(args),
            out_specs=(pl.BlockSpec(memory_space=space),) * len(outs),
            scratch_shapes=scratch,
            name=name,
        )(pos, *args)

    return run


def greet(nr, nc, between=None):
    r, c = lax.axis_index("row"), lax.axis_index("col")
    barrier = pltpu.get_barrier_semaphore()
    for k in range(1, nc):
        pl.semaphore_signal(barrier, inc=1, device_id=(r, (c + k) % nc), device_id_type=MESH)
    for k in range(1, nr):
        pl.semaphore_signal(barrier, inc=1, device_id=((r + k) % nr, c), device_id_type=MESH)
    if between is not None:
        between(r, c)
    pl.semaphore_wait(barrier, nr + nc - 2)
    return r, c


def turn(a, block, out):
    for k in range(a.shape[1] // BAND):
        at = pl.ds(k * BAND, BAND)
        out[at, :] = a[pl.ds(block * BAND, BAND), at].T


def rows_at(index, size):
    return pl.ds(pl.multiple_of(index * size, 8), size)


class Spread:
    def __init__(self, axis, parts, me, other, dst, sems):
        self.axis, self.parts, self.me, self.other, self.dst = axis, parts, me, other, dst
        self.root_send, self.root_recv, self.send, self.recv = sems
        self.size = dst.shape[0] // parts

    def device(self, k):
        return (self.other, k) if self.axis == "col" else (k, self.other)

    def copy(self, k, src):
        rows = pl.ds(k * self.size, self.size)
        return pltpu.make_async_remote_copy(
            src_ref=src(rows),
            dst_ref=self.dst.at[rows],
            send_sem=self.root_send.at[k],
            recv_sem=self.root_recv,
            device_id=self.device(k),
            device_id_type=MESH,
        )

    def scatter(self, src):
        @pl.when(self.me == 0)
        def _():
            for k in range(1, self.parts):
                self.copy(k, src).start()
            rows = pl.ds(0, self.size)
            self.dst[rows, :] = src(rows)[...]

    def gather(self, src):
        @pl.when(self.me != 0)
        def _():
            self.copy(1, src).wait_recv()

        self.copies = []
        for k in range(1, self.parts):
            rows = rows_at(self.me, self.size)
            copy = pltpu.make_async_remote_copy(
                src_ref=self.dst.at[rows],
                dst_ref=self.dst.at[rows],
                send_sem=self.send.at[k],
                recv_sem=self.recv.at[k],
                device_id=self.device((self.me + k) % self.parts),
                device_id_type=MESH,
            )
            copy.start()
            self.copies.append(copy)

    def finish(self, src):
        for copy in self.copies:
            copy.wait()

        @pl.when(self.me == 0)
        def _():
            for k in range(1, self.parts):
                self.copy(k, src).wait_send()


def spread_sems(parts):
    dma = pltpu.SemaphoreType.DMA
    return [dma((parts,)), dma, dma((parts,)), dma((parts,))]


def spread_kernel(nr, nc, a, pr, pc, ts, xr, xc, t, *sems):
    rows_sems, cols_sems, (send, recv, down_send, down_recv) = sems[:4], sems[4:8], sems[8:]
    b = BAND

    def prepare(r, c):
        @pl.when(c == 0)
        def _():
            xr[...] = a[:, 0:b]

        @pl.when(r == 0)
        def _():
            turn(a, 0, xc)

        @pl.when((r == 0) & (c == 0))
        def _():
            xr[0:b, :] = jnp.zeros((b, b), jnp.float32)
            xc[0:b, :] = jnp.zeros((b, b), jnp.float32)
            rows = b // nc
            for k, (i, j) in enumerate(((1, 0), (1, 1), (2, 0), (2, 1), (2, 2), (0, 2), (1, 2))):
                block = a[i * b : (i + 1) * b, j * b : (j + 1) * b]
                t[:, k * rows : (k + 1) * rows, :] = block.reshape(nc, rows, b)

    r, c = greet(nr, nc, prepare)
    rows = Spread("col", nc, c, r, pr, rows_sems)
    cols = Spread("row", nr, r, c, pc, cols_sems)
    rows.scatter(lambda at: xr.at[at])
    cols.scatter(lambda at: xc.at[at])

    def slice_to(k):
        return pltpu.make_async_remote_copy(
            src_ref=t.at[k], dst_ref=ts, send_sem=send.at[k], recv_sem=recv, device_id=(r, k), device_id_type=MESH
        )

    def down(k):
        return pltpu.make_async_remote_copy(
            src_ref=ts, dst_ref=ts, send_sem=down_send.at[k], recv_sem=down_recv, device_id=(k, c), device_id_type=MESH
        )

    @pl.when((r == 0) & (c == 0))
    def _():
        for k in range(1, nc):
            slice_to(k).start()
        ts[...] = t[0]

    rows.gather(lambda at: xr.at[at])
    cols.gather(lambda at: xc.at[at])

    @pl.when((r == 0) & (c != 0))
    def _():
        slice_to(1).wait_recv()

    @pl.when(r == 0)
    def _():
        for k in range(1, nr):
            down(k).start()

    @pl.when(r != 0)
    def _():
        down(1).wait_recv()

    rows.finish(lambda at: xr.at[at])
    cols.finish(lambda at: xc.at[at])

    @pl.when(r == 0)
    def _():
        for k in range(1, nr):
            down(k).wait_send()

    @pl.when((r == 0) & (c == 0))
    def _():
        for k in range(1, nc):
            slice_to(k).wait_send()


def middle_kernel(
    nr, nc, first, count, gather, a, pr, pc, t, cinv, rinv, f, ft, finv, finvt, out_r, out_c, out_h, er, ec, *rest
):
    out_t, rest = (rest[0], rest[1:]) if gather else (None, rest)
    sr, sc, h, gram, part_r, part_c, part_h, part_g, sum_r, sum_c, sum_h, sum_g, all_g, cols_h, all_h, xc = rest[:16]
    send, recv, *sems = rest[16:]
    b = BAND
    n = a.shape[0]
    size_r, size_c, size_h, size_g = n // nc, n // nr, h.shape[0] // nc, b // nc

    def prepare(r, c):
        @pl.when(r >= 0)
        def _():
            gram[...] = mm(pr[...], pr[...], 0, 0)
            part_g[r] = gram[rows_at(c, size_g), :]

        @pl.when(r == 0)
        def _():
            turn(a, first, xc)

    r, c = greet(nr, nc, prepare)
    always = r >= 0

    def along(axis, phase, source, target):
        parts, me = (nc, c) if axis == "col" else (nr, r)
        copies = []
        for k in range(1, parts):
            to = (me + k) % parts
            copy = pltpu.make_async_remote_copy(
                src_ref=source(to),
                dst_ref=target(k),
                send_sem=send.at[phase, k],
                recv_sem=recv.at[phase, k],
                device_id=(r, to) if axis == "col" else (to, c),
                device_id_type=MESH,
            )
            copy.start()
            copies.append(copy)
        return copies

    def finish(copies):
        for copy in copies:
            copy.wait()

    def block(body):
        pl.when(always)(body)

    g_copies = along("row", 0, lambda to: gram.at[rows_at(c, size_g)], lambda k: part_g.at[r])
    t_copies = []
    if gather:
        t_copies = along("col", 1, lambda to: t, lambda k: out_t.at[c])
        out_t[c] = t[...]
    rows = Spread("col", nc, c, r, er, sems[:4])
    cols = Spread("row", nr, r, c, ec, sems[4:])
    rows_src = lambda at: a.at[at, first * b : (first + 1) * b]
    cols_src = lambda at: xc.at[at]
    rows.scatter(rows_src)
    cols.scatter(cols_src)

    tile = 2 * b if n % (2 * b) == 0 else b

    @pl.loop(0, n // tile)
    def _(step):
        at = pl.ds(pl.multiple_of(step * tile, tile), tile)
        sr[at, :] = dot(a[at, :], pc[...])

    r_copies = along("col", 2, lambda to: sr.at[rows_at(to, size_r)], lambda k: part_r.at[k])

    finish(g_copies)
    value = part_g[0]
    for k in range(1, nr):
        value = value + part_g[k]
    sum_g[...] = value
    all_g[c] = value
    g_copies = along("col", 3, lambda to: sum_g, lambda k: all_g.at[c])

    @block
    def _():
        h[0:b, :] = mm(pr[...], sr[...], 0, 0)
        h[b : (1 + count) * b, :] = jnp.where(r == 0, sr[first * b : (first + count) * b, :], 0.0)

    h_copies = along("col", 4, lambda to: h.at[rows_at(to, size_h)], lambda k: part_h.at[k])

    @pl.loop(0, n // tile)
    def _(step):
        at = pl.ds(pl.multiple_of(step * tile, tile), tile)
        sc[at, :] = mm(a[:, at], pr[...], 0, 0)

    c_copies = along("row", 5, lambda to: sc.at[rows_at(to, size_c)], lambda k: part_c.at[k])
    rows.gather(rows_src)
    cols.gather(cols_src)
    finish(g_copies)

    @block
    def _():
        invert_chol(whole(all_g), cinv, rinv)

    finish(h_copies)
    value = h[rows_at(c, size_h), :]
    for k in range(1, nc):
        value = value + part_h[k]
    sum_h[...] = value
    cols_h[r] = value
    h_copies = along("row", 6, lambda to: sum_h, lambda k: cols_h.at[r])

    finish(r_copies)
    value = sr[rows_at(c, size_r), :]
    for k in range(1, nc):
        value = value + part_r[k]
    sum_r[...] = value
    out_r[rows_at(c, size_r), :] = value
    r_copies = along("col", 7, lambda to: sum_r, lambda k: out_r.at[rows_at(c, size_r)])

    finish(c_copies)
    value = sc[rows_at(r, size_c), :]
    for k in range(1, nr):
        value = value + part_c[k]
    sum_c[...] = value
    out_c[rows_at(r, size_c), :] = value
    c_copies = along("row", 8, lambda to: sum_c, lambda k: out_c.at[rows_at(r, size_c)])
    finish(t_copies)

    @block
    def _():
        invert_top(piece(out_t, 0) if gather else t[...], rinv, f, ft, finv, finvt)

    finish(h_copies)
    value = cols_h[0]
    for k in range(1, nr):
        value = value + cols_h[k]
    all_h[...] = value
    out_h[rows_at(c, size_h), :] = value
    h_copies = along("col", 9, lambda to: all_h, lambda k: out_h.at[rows_at(c, size_h)])
    for copies in (r_copies, c_copies, h_copies):
        finish(copies)
    rows.finish(rows_src)
    cols.finish(cols_src)


def spread(nr, nc, a):
    dma = pltpu.SemaphoreType.DMA
    b = BAND
    n = a.shape[0]
    tops = 7 * b // nc
    return pl.pallas_call(
        functools.partial(spread_kernel, nr, nc),
        out_shape=tuple(jax.ShapeDtypeStruct(s, jnp.float32) for s in ((n, b), (n, b), (tops, b))),
        in_specs=[pl.BlockSpec(memory_space=VMEM)],
        out_specs=(pl.BlockSpec(memory_space=VMEM),) * 3,
        scratch_shapes=[
            *(VMEM(s, jnp.float32) for s in ((n, b), (n, b), (nc, tops, b))),
            *spread_sems(nc), *spread_sems(nr), dma((nc,)), dma, dma((nr,)), dma,
        ],
        compiler_params=pltpu.CompilerParams(collective_id=0, has_side_effects=True),
        name="spread",
    )(a)


def middle(nr, nc, first, count, gather, a, pr, pc, t):
    most = max(nr, nc)
    dma = pltpu.SemaphoreType.DMA
    b = BAND
    n = a.shape[0]
    heads = (1 + count) * b
    size_r, size_c, size_h, size_g = n // nc, n // nr, heads // nc, b // nc
    outs = [(b, b)] * 6 + [(n, b), (n, b), (heads, b), (n, b), (n, b)]
    if gather:
        outs.append((nc, *t.shape))
    scratch = [
        (n, b), (n, b), (heads, b), (b, b),
        (nc, size_r, b), (nr, size_c, b), (nc, size_h, b), (nr, size_g, b),
        (size_r, b), (size_c, b), (size_h, b), (size_g, b), (nc, size_g, b), (nr, size_h, b), (size_h, b), (n, b),
    ]
    return pl.pallas_call(
        functools.partial(middle_kernel, nr, nc, first, count, gather),
        out_shape=tuple(jax.ShapeDtypeStruct(s, jnp.float32) for s in outs),
        in_specs=[pl.BlockSpec(memory_space=VMEM)] * 4,
        out_specs=(pl.BlockSpec(memory_space=VMEM),) * len(outs),
        scratch_shapes=[
            *(VMEM(s, jnp.float32) for s in scratch),
            dma((10, most)), dma((10, most)), *spread_sems(nc), *spread_sems(nr),
        ],
        compiler_params=pltpu.CompilerParams(collective_id=first, has_side_effects=True),
        name=f"middle_{first}",
    )(a, pr, pc, t)


def shards(nr, nc, matrix):
    n = matrix.shape[0]
    b = BAND
    row, col = lax.axis_index("row"), lax.axis_index("col")
    pos = jnp.stack([row, col]).astype(jnp.int32)
    vmem = lambda *shape: VMEM(shape, jnp.float32)
    p1r, p1c, t = spread(nr, nc, matrix)
    *fac, sr, sc, h, er, ec, t = middle(nr, nc, 1, 2, True, matrix, p1r, p1c, t)
    one = call(
        step_one_kernel,
        [(n, n), (n, b), (n, b), (b, b), (b, b)],
        "step_one",
        [vmem(n, 2 * b), vmem(n, 2 * b), vmem(b, 3 * b), vmem(7, b, b)],
    )
    updated, p2r, p2c, t2, a33 = one(pos, *fac, h, t, p1r, sr, er, p1c, sc, ec, matrix)
    *fac, sr, sc, h, er, ec = middle(nr, nc, 2, 1, False, updated, p2r, p2c, t2)
    two = call(
        step_two_kernel,
        [(n, n)],
        "step_two",
        [vmem(n, 2 * b), vmem(n, 2 * b), vmem(b, b), vmem(b, b), vmem(n, n), pltpu.SemaphoreType.DMA((n // b,))],
        pl.ANY,
    )
    return two(pos, *fac, h, a33, p2r, sr, er, p2c, sc, ec, updated)[0]


def solution(mesh):
    spec = P("row", "col")
    body = functools.partial(shards, mesh.shape["row"], mesh.shape["col"])
    return jax.shard_map(body, mesh=mesh, in_specs=(spec,), out_specs=spec, check_vma=False)
```

```python
import functools

import jax
import jax.numpy as jnp
from jax import lax
from jax.experimental import pallas as pl
from jax.experimental.pallas import tpu as pltpu
from jax.sharding import PartitionSpec as P

BAND = 128
HIGH = lax.Precision.HIGHEST
VMEM = pltpu.VMEM
MESH = pl.DeviceIdType.MESH


def dot(left, right):
    return jnp.dot(left, right, precision=HIGH, preferred_element_type=jnp.float32)


def mm(left, right, ca=1, cb=0):
    return lax.dot_general(
        left, right, (((ca,), (cb,)), ((), ())), precision=HIGH, preferred_element_type=jnp.float32
    )


def eliminate(x_ref, jordan):
    n = x_ref.shape[0]
    lane = lax.broadcasted_iota(jnp.int32, (1, n), 1)
    rows = lax.broadcasted_iota(jnp.int32, (n, 1), 0)
    rows8 = lax.broadcasted_iota(jnp.int32, (8, n), 0)
    lane8 = lax.broadcasted_iota(jnp.int32, (8, n), 1)

    def block(j, _):
        at = pl.ds(pl.multiple_of(8 * j, 8), 8)
        full = x_ref[...]
        strip = x_ref[at, :]
        cols = [jnp.broadcast_to(strip[:, i : i + 1], (8, n)) for i in range(8)]
        kept = strip
        for i in range(8):
            if not jordan:
                kept = jnp.where(rows8 == i, strip, kept)
            inv = 1.0 / jnp.broadcast_to(cols[i][i : i + 1, :], (8, n))
            mult = jnp.where(rows8 == i, -inv, cols[i] * inv)
            for k in range(i + 1, 8):
                cols[k] = jnp.where(rows8 == i, 0.0, cols[k]) - mult * cols[k][i : i + 1, :]
            row = jnp.where(lane == i, 1.0, strip[i : i + 1, :])
            strip = jnp.where((rows8 == i) | (lane8 == i), 0.0, strip) - mult * row
        ids = rows - 8 * j
        out = jnp.where(lane < 8, 0.0, full)
        for i in range(8):
            out = out - full[:, i : i + 1] * strip[i : i + 1, :]
        if jordan:
            x_ref[...] = pltpu.roll(out, n - 8, 1)
            x_ref[at, :] = pltpu.roll(strip, n - 8, 1)
        else:
            x_ref[...] = pltpu.roll(jnp.where(ids >= 8, out, full), n - 8, 1)
            x_ref[at, :] = pltpu.roll(kept, n - 8, 1)
        return 0

    lax.fori_loop(0, n // 8, block, 0)


def piece(ref, k):
    parts, _, n = ref.shape
    rows = BAND // parts
    return ref[:, k * rows : (k + 1) * rows, :].reshape(BAND, n)


def whole(ref):
    parts, rows, n = ref.shape
    return ref[...].reshape(parts * rows, n)


def invert_chol(gram, cinv_ref, rinv_ref):
    n = BAND
    r = lax.broadcasted_iota(jnp.int32, (n, n), 0)
    c = lax.broadcasted_iota(jnp.int32, (n, n), 1)
    cinv_ref[...] = gram
    eliminate(cinv_ref, False)
    x = cinv_ref[...]
    diag = jnp.sum(jnp.where(r == c, x, 0.0), axis=1, keepdims=True)
    cinv = jnp.where(r > c, x, (r == c).astype(jnp.float32)) / jnp.sqrt(diag)
    cinv_ref[...] = cinv
    rinv_ref[...] = cinv.T


def invert_top(top, rinv_ref, f_ref, ft_ref, finv_ref, finvt_ref):
    n = BAND
    r = lax.broadcasted_iota(jnp.int32, (n, n), 0)
    c = lax.broadcasted_iota(jnp.int32, (n, n), 1)
    f = dot(top, rinv_ref[...]) + (r == c).astype(jnp.float32)
    f_ref[...] = f
    ft_ref[...] = f.T
    finv_ref[...] = f
    eliminate(finv_ref, True)
    finvt_ref[...] = finv_ref[...].T


def weights(fac, h, s_top, s_topt, a_ss):
    cinv, rinv, _, _, finv, finvt = fac
    half = dot(cinv, h) + s_top
    j = dot(half, rinv) + dot(cinv, s_topt) + a_ss
    return dot(dot(finv, j), finvt)


def step_one_kernel(
    pos_ref, cinv_ref, rinv_ref, f_ref, ft_ref, finv_ref, finvt_ref, h_ref, g_ref,
    pr_ref, sr_ref, er_ref, pc_ref, sc_ref, ec_ref, a_ref,
    updated_ref, p2r_ref, p2c_ref, t2_ref, a33_ref, left_ref, right_ref, ht_ref, small_ref,
):
    b = BAND
    n = pr_ref.shape[0]
    always = pos_ref[0] >= 0
    sums = lambda k: h_ref[k * b : (k + 1) * b, :]
    sumst = lambda k: ht_ref[:, k * b : (k + 1) * b]

    @pl.when(always)
    def _():
        for k in range(3):
            ht_ref[:, k * b : (k + 1) * b] = h_ref[k * b : (k + 1) * b, :].T

    a22, a31, a32, a33, a13, a23 = (functools.partial(piece, g_ref, k) for k in range(1, 7))

    @pl.when(always)
    def _():
        fac = tuple(ref[...] for ref in (cinv_ref, rinv_ref, f_ref, ft_ref, finv_ref, finvt_ref))
        small_ref[0, :, :] = weights(fac, sums(0), sums(1), sumst(1), a22())

    @pl.when(always)
    def _():
        small_ref[6, :, :] = dot(a31(), rinv_ref[...])
        small_ref[3, :, :] = dot(cinv_ref[...], a13())

    def work(slot, house, sums, cols):
        @pl.when(always)
        def _():
            rows = dot(dot(sums, rinv_ref[...]) + cols(), finvt_ref[...])
            small_ref[slot, :, :] = rows - 0.5 * dot(house(), small_ref[0])

    def workt(slot, house, sums, cols):
        @pl.when(always)
        def _():
            rows = dot(finv_ref[...], dot(cinv_ref[...], sums) + cols())
            small_ref[slot, :, :] = rows - 0.5 * dot(small_ref[0], house())

    work(5, lambda: small_ref[6], sums(2), a32)
    work(4, lambda: f_ref[...], sums(1), a22)
    workt(1, lambda: ft_ref[...], sumst(1), a22)
    workt(2, lambda: small_ref[3], sumst(2), a23)

    @pl.when(always)
    def _():
        t2_ref[...] = a32() - dot(small_ref[6], small_ref[1]) - dot(small_ref[5], ft_ref[...])
        a33_ref[...] = a33() - dot(small_ref[6], small_ref[2]) - dot(small_ref[5], small_ref[3])

    tile = 2 * b if n % (2 * b) == 0 else b

    def side(start, p_ref, s_ref, e_ref, out_ref, house_at, work_at, p2_ref):
        @pl.loop(0, n // tile)
        def _(step):
            at = pl.ds(pl.multiple_of(step * tile, tile), tile)
            ids = start * n + step * tile + lax.broadcasted_iota(jnp.int32, (tile, b), 0)
            lane = lax.broadcasted_iota(jnp.int32, (tile, b), 1)
            house = dot(p_ref[at, :], rinv_ref[...]) + (ids - b == lane).astype(jnp.float32)
            cols = e_ref[at, :]
            wk = dot(dot(s_ref[at, :], rinv_ref[...]) + cols, finvt_ref[...]) - 0.5 * dot(house, small_ref[0])
            out_ref[at, house_at : house_at + b] = house
            out_ref[at, work_at : work_at + b] = wk
            p2 = cols - dot(house, small_ref[1]) - dot(wk, ft_ref[...])
            p2_ref[at, :] = jnp.where(ids >= 2 * b, p2, 0.0)

    side(pos_ref[0], pr_ref, sr_ref, er_ref, left_ref, 0, b, p2r_ref)
    side(pos_ref[1], pc_ref, sc_ref, ec_ref, right_ref, b, 0, p2c_ref)

    @pl.loop(0, n // tile)
    def _(step):
        at = pl.ds(pl.multiple_of(step * tile, tile), tile)
        updated_ref[at, :] = a_ref[at, :] - mm(left_ref[at, :], right_ref[...], 1, 1)


def step_two_kernel(
    pos_ref, cinv_ref, rinv_ref, f_ref, ft_ref, finv_ref, finvt_ref, h_ref, a33_ref,
    pr_ref, sr_ref, er_ref, pc_ref, sc_ref, ec_ref, a_ref,
    out_ref, left_ref, right_ref, ht_ref, z_ref, result_ref, sem,
):
    b = BAND
    n = pr_ref.shape[0]
    tile = 2 * b if n % (2 * b) == 0 else b

    @pl.when(pos_ref[0] >= 0)
    def _():
        ht_ref[...] = h_ref[b : 2 * b, :].T

    @pl.when(pos_ref[0] >= 0)
    def _():
        fac = tuple(ref[...] for ref in (cinv_ref, rinv_ref, f_ref, ft_ref, finv_ref, finvt_ref))
        z_ref[...] = weights(fac, h_ref[0:b, :], h_ref[b : 2 * b, :], ht_ref[...], a33_ref[...])

    def side(start, p_ref, s_ref, e_ref, out_ref, house_at, work_at):
        @pl.loop(0, n // tile)
        def _(step):
            at = pl.ds(pl.multiple_of(step * tile, tile), tile)
            ids = start * n + step * tile + lax.broadcasted_iota(jnp.int32, (tile, b), 0)
            lane = lax.broadcasted_iota(jnp.int32, (tile, b), 1)
            house = dot(p_ref[at, :], rinv_ref[...]) + (ids - 2 * b == lane).astype(jnp.float32)
            out_ref[at, house_at : house_at + b] = house
            ay = dot(s_ref[at, :], rinv_ref[...]) + e_ref[at, :]
            out_ref[at, work_at : work_at + b] = dot(ay, finvt_ref[...]) - 0.5 * dot(house, z_ref[...])

    side(pos_ref[0], pr_ref, sr_ref, er_ref, left_ref, 0, b)
    side(pos_ref[1], pc_ref, sc_ref, ec_ref, right_ref, b, 0)

    def store(step):
        at = pl.ds(pl.multiple_of(step * tile, tile), tile)
        return pltpu.make_async_copy(result_ref.at[at], out_ref.at[at], sem.at[step])

    @pl.loop(0, n // tile)
    def _(step):
        at = pl.ds(pl.multiple_of(step * tile, tile), tile)
        result_ref[at, :] = a_ref[at, :] - mm(left_ref[at, :], right_ref[...], 1, 1)
        store(step).start()

    @pl.loop(0, n // tile)
    def _(step):
        store(step).wait()


def call(body, outs, name, scratch, space=VMEM):
    def run(pos, *args):
        return pl.pallas_call(
            body,
            out_shape=tuple(jax.ShapeDtypeStruct(s, jnp.float32) for s in outs),
            in_specs=[pl.BlockSpec(memory_space=pltpu.SMEM)] + [pl.BlockSpec(memory_space=VMEM)] * len(args),
            out_specs=(pl.BlockSpec(memory_space=space),) * len(outs),
            scratch_shapes=scratch,
            name=name,
        )(pos, *args)

    return run


def greet(nr, nc, between=None):
    r, c = lax.axis_index("row"), lax.axis_index("col")
    barrier = pltpu.get_barrier_semaphore()
    for k in range(1, nc):
        pl.semaphore_signal(barrier, inc=1, device_id=(r, (c + k) % nc), device_id_type=MESH)
    for k in range(1, nr):
        pl.semaphore_signal(barrier, inc=1, device_id=((r + k) % nr, c), device_id_type=MESH)
    if between is not None:
        between(r, c)
    pl.semaphore_wait(barrier, nr + nc - 2)
    return r, c


def turn(a, block, out):
    for k in range(a.shape[1] // BAND):
        at = pl.ds(k * BAND, BAND)
        out[at, :] = a[pl.ds(block * BAND, BAND), at].T


def rows_at(index, size):
    return pl.ds(pl.multiple_of(index * size, 8), size)


class Spread:
    def __init__(self, axis, parts, me, other, dst, sems, pair_sems=None):
        self.pair = None if pair_sems is None else PairGather(me, other, parts, dst, pair_sems)
        self.axis, self.parts, self.me, self.other, self.dst = axis, parts, me, other, dst
        self.root_send, self.root_recv, self.send, self.recv = sems
        self.size = dst.shape[0] // parts

    def device(self, k):
        return (self.other, k) if self.axis == "col" else (k, self.other)

    def copy(self, k, src):
        rows = pl.ds(k * self.size, self.size)
        return pltpu.make_async_remote_copy(
            src_ref=src(rows),
            dst_ref=self.dst.at[rows],
            send_sem=self.root_send.at[k],
            recv_sem=self.root_recv,
            device_id=self.device(k),
            device_id_type=MESH,
        )

    def scatter(self, src):
        @pl.when(self.me == 0)
        def _():
            for k in range(1, self.parts):
                self.copy(k, src).start()
            rows = pl.ds(0, self.size)
            self.dst[rows, :] = src(rows)[...]

    def gather(self, src):
        @pl.when(self.me != 0)
        def _():
            self.copy(1, src).wait_recv()

        self.copies = []
        if self.pair is not None:
            self.pair.start()
            return
        for k in range(1, self.parts):
            rows = rows_at(self.me, self.size)
            copy = pltpu.make_async_remote_copy(
                src_ref=self.dst.at[rows],
                dst_ref=self.dst.at[rows],
                send_sem=self.send.at[k],
                recv_sem=self.recv.at[k],
                device_id=self.device((self.me + k) % self.parts),
                device_id_type=MESH,
            )
            copy.start()
            self.copies.append(copy)

    def finish(self, src):
        for copy in self.copies:
            copy.wait()
        if self.pair is not None:
            self.pair.finish()

        @pl.when(self.me == 0)
        def _():
            for k in range(1, self.parts):
                self.copy(k, src).wait_send()


class PairGather:
    def __init__(self, r, c, nr, dst, sems):
        self.r, self.c, self.count, self.dst = r, c, nr // 2, dst
        self.z, self.p = r // 2, r % 2
        self.sems = sems
        self.size = dst.shape[0] // nr

    def copy(self, src, index, to, stage, k):
        return pltpu.make_async_remote_copy(
            src_ref=src,
            dst_ref=self.dst.at[rows_at(index, self.size)],
            send_sem=self.sems[2 * stage].at[k],
            recv_sem=self.sems[2 * stage + 1].at[k],
            device_id=(to, self.c),
            device_id_type=MESH,
        )

    def start(self, src=None):
        src = self.dst.at[rows_at(self.r, self.size)] if src is None else src
        self.partner = 2 * self.z + 1 - self.p
        self.far = []
        for k in range(1, self.count):
            to = 2 * ((self.z + k) % self.count) + self.p
            self.far.append(self.copy(src, self.r, to, 0, k))
        for copy in self.far:
            copy.start()
        self.near = [self.copy(src, self.r, self.partner, 1, 0)]
        self.near[0].start()

    def forward(self):
        for k in sorted(range(1, self.count), key=lambda k: min(k, self.count - k)):
            self.far[k - 1].wait_recv()
            index = 2 * ((self.z + self.count - k) % self.count) + self.p
            copy = self.copy(self.dst.at[rows_at(index, self.size)], index, self.partner, 1, k)
            copy.start()
            self.near.append(copy)

    def finish(self):
        for copy in self.far:
            copy.wait_send()
        for copy in self.near:
            copy.wait()


def pair_sems(nr):
    return [pltpu.SemaphoreType.DMA((nr // 2,)) for _ in range(4)]


def spread_sems(parts):
    dma = pltpu.SemaphoreType.DMA
    return [dma((parts,)), dma, dma((parts,)), dma((parts,))]


def spread_kernel(nr, nc, a, pr, pc, ts, xr, xc, t, *sems):
    rows_sems, cols_sems, (send, recv, down_send, down_recv) = sems[:4], sems[4:8], sems[8:12]
    b = BAND

    def prepare(r, c):
        @pl.when(c == 0)
        def _():
            xr[...] = a[:, 0:b]

        @pl.when(r == 0)
        def _():
            turn(a, 0, xc)

        @pl.when((r == 0) & (c == 0))
        def _():
            xr[0:b, :] = jnp.zeros((b, b), jnp.float32)
            xc[0:b, :] = jnp.zeros((b, b), jnp.float32)
            rows = b // nc
            for k, (i, j) in enumerate(((1, 0), (1, 1), (2, 0), (2, 1), (2, 2), (0, 2), (1, 2))):
                block = a[i * b : (i + 1) * b, j * b : (j + 1) * b]
                t[:, k * rows : (k + 1) * rows, :] = block.reshape(nc, rows, b)

    r, c = greet(nr, nc, prepare)
    rows = Spread("col", nc, c, r, pr, rows_sems)
    cols = Spread("row", nr, r, c, pc, cols_sems, sems[12:])
    rows.scatter(lambda at: xr.at[at])
    cols.scatter(lambda at: xc.at[at])

    def slice_to(k):
        return pltpu.make_async_remote_copy(
            src_ref=t.at[k], dst_ref=ts, send_sem=send.at[k], recv_sem=recv, device_id=(r, k), device_id_type=MESH
        )

    def down(k):
        return pltpu.make_async_remote_copy(
            src_ref=ts, dst_ref=ts, send_sem=down_send.at[k], recv_sem=down_recv, device_id=(k, c), device_id_type=MESH
        )

    @pl.when((r == 0) & (c == 0))
    def _():
        for k in range(1, nc):
            slice_to(k).start()
        ts[...] = t[0]

    rows.gather(lambda at: xr.at[at])
    cols.gather(lambda at: xc.at[at])

    @pl.when((r == 0) & (c != 0))
    def _():
        slice_to(1).wait_recv()

    @pl.when(r == 0)
    def _():
        for k in range(1, nr):
            down(k).start()

    cols.pair.forward()

    @pl.when(r != 0)
    def _():
        down(1).wait_recv()

    rows.finish(lambda at: xr.at[at])
    cols.finish(lambda at: xc.at[at])

    @pl.when(r == 0)
    def _():
        for k in range(1, nr):
            down(k).wait_send()

    @pl.when((r == 0) & (c == 0))
    def _():
        for k in range(1, nc):
            slice_to(k).wait_send()


def middle_kernel(
    nr, nc, first, count, gather, a, pr, pc, t, cinv, rinv, f, ft, finv, finvt, out_r, out_c, out_h, er, ec, *rest
):
    out_t, rest = (rest[0], rest[1:]) if gather else (None, rest)
    sr, sc, h, gram, part_r, part_c, part_h, part_g, sum_r, sum_c, sum_h, sum_g, all_g, cols_h, all_h, xc, part_p, sum_p = rest[:18]
    send, recv, *sems = rest[18:]
    b = BAND
    n = a.shape[0]
    size_r, size_c, size_h, size_g = n // nc, n // nr, h.shape[0] // nc, b // nc

    def prepare(r, c):
        @pl.when(r >= 0)
        def _():
            gram[...] = mm(pr[...], pr[...], 0, 0)
            part_g[r] = gram[rows_at(c, size_g), :]

        @pl.when(r == 0)
        def _():
            turn(a, first, xc)

    r, c = greet(nr, nc, prepare)
    always = r >= 0

    def along(axis, phase, source, target):
        parts, me = (nc, c) if axis == "col" else (nr, r)
        copies = []
        for k in range(1, parts):
            to = (me + k) % parts
            copy = pltpu.make_async_remote_copy(
                src_ref=source(to),
                dst_ref=target(k),
                send_sem=send.at[phase, k],
                recv_sem=recv.at[phase, k],
                device_id=(r, to) if axis == "col" else (to, c),
                device_id_type=MESH,
            )
            copy.start()
            copies.append(copy)
        return copies

    def finish(copies):
        for copy in copies:
            copy.wait()

    def block(body):
        pl.when(always)(body)

    g_copies = along("row", 0, lambda to: gram.at[rows_at(c, size_g)], lambda k: part_g.at[r])
    t_copies = []
    if gather:
        t_copies = along("col", 1, lambda to: t, lambda k: out_t.at[c])
        out_t[c] = t[...]
    rows = Spread("col", nc, c, r, er, sems[:4])
    cols = Spread("row", nr, r, c, ec, sems[4:8], sems[8:12])
    gather_c = PairGather(r, c, nr, out_c, sems[12:])
    rows_src = lambda at: a.at[at, first * b : (first + 1) * b]
    cols_src = lambda at: xc.at[at]
    rows.scatter(rows_src)
    cols.scatter(cols_src)

    tile = 2 * b if n % (2 * b) == 0 else b

    @pl.loop(0, n // tile)
    def _(step):
        at = pl.ds(pl.multiple_of(step * tile, tile), tile)
        sr[at, :] = dot(a[at, :], pc[...])

    r_copies = along("col", 2, lambda to: sr.at[rows_at(to, size_r)], lambda k: part_r.at[k])

    finish(g_copies)
    value = part_g[0]
    for k in range(1, nr):
        value = value + part_g[k]
    sum_g[...] = value
    all_g[c] = value
    g_copies = along("col", 3, lambda to: sum_g, lambda k: all_g.at[c])

    @pl.loop(0, n // tile)
    def _(step):
        at = pl.ds(pl.multiple_of(step * tile, tile), tile)
        sc[at, :] = mm(a[:, at], pr[...], 0, 0)

    z, p = r // 2, r % 2
    half = nr // 2
    p_copies = []
    for i in range(half):
        copy = pltpu.make_async_remote_copy(
            src_ref=sc.at[rows_at(2 * i + 1 - p, size_c)],
            dst_ref=part_p.at[i],
            send_sem=send.at[5, i],
            recv_sem=recv.at[5, i],
            device_id=(2 * z + 1 - p, c),
            device_id_type=MESH,
        )
        copy.start()
        p_copies.append(copy)

    @block
    def _():
        h[0:b, :] = mm(pr[...], sr[...], 0, 0)
        h[b : (1 + count) * b, :] = jnp.where(r == 0, sr[first * b : (first + count) * b, :], 0.0)

    h_copies = along("col", 4, lambda to: h.at[rows_at(to, size_h)], lambda k: part_h.at[k])
    finish(p_copies)
    for i in range(half):
        sum_p[i] = sc[rows_at(2 * i + p, size_c), :] + part_p[i]
    c_copies = []
    for k in range(1, half):
        to = (z + k) % half
        copy = pltpu.make_async_remote_copy(
            src_ref=sum_p.at[to],
            dst_ref=part_c.at[k],
            send_sem=send.at[8, k],
            recv_sem=recv.at[8, k],
            device_id=(2 * to + p, c),
            device_id_type=MESH,
        )
        copy.start()
        c_copies.append(copy)
    rows.gather(rows_src)
    cols.gather(cols_src)
    finish(g_copies)

    @block
    def _():
        invert_chol(whole(all_g), cinv, rinv)

    finish(h_copies)
    value = h[rows_at(c, size_h), :]
    for k in range(1, nc):
        value = value + part_h[k]
    sum_h[...] = value
    cols_h[r] = value
    h_copies = along("row", 6, lambda to: sum_h, lambda k: cols_h.at[r])

    finish(r_copies)
    value = sr[rows_at(c, size_r), :]
    for k in range(1, nc):
        value = value + part_r[k]
    sum_r[...] = value
    out_r[rows_at(c, size_r), :] = value
    r_copies = along("col", 7, lambda to: sum_r, lambda k: out_r.at[rows_at(c, size_r)])

    finish(c_copies)
    value = sum_p[z]
    for k in range(1, half):
        value = value + part_c[k]
    sum_c[...] = value
    out_c[rows_at(r, size_c), :] = value
    gather_c.start(sum_c)
    finish(t_copies)

    @block
    def _():
        invert_top(piece(out_t, 0) if gather else t[...], rinv, f, ft, finv, finvt)

    finish(h_copies)
    value = cols_h[0]
    for k in range(1, nr):
        value = value + cols_h[k]
    all_h[...] = value
    out_h[rows_at(c, size_h), :] = value
    h_copies = along("col", 9, lambda to: all_h, lambda k: out_h.at[rows_at(c, size_h)])
    gather_c.forward()
    cols.pair.forward()
    for copies in (r_copies, h_copies):
        finish(copies)
    gather_c.finish()
    rows.finish(rows_src)
    cols.finish(cols_src)


def spread(nr, nc, a):
    dma = pltpu.SemaphoreType.DMA
    b = BAND
    n = a.shape[0]
    tops = 7 * b // nc
    return pl.pallas_call(
        functools.partial(spread_kernel, nr, nc),
        out_shape=tuple(jax.ShapeDtypeStruct(s, jnp.float32) for s in ((n, b), (n, b), (tops, b))),
        in_specs=[pl.BlockSpec(memory_space=VMEM)],
        out_specs=(pl.BlockSpec(memory_space=VMEM),) * 3,
        scratch_shapes=[
            *(VMEM(s, jnp.float32) for s in ((n, b), (n, b), (nc, tops, b))),
            *spread_sems(nc), *spread_sems(nr), dma((nc,)), dma, dma((nr,)), dma, *pair_sems(nr),
        ],
        compiler_params=pltpu.CompilerParams(collective_id=0, has_side_effects=True),
        name="spread",
    )(a)


def middle(nr, nc, first, count, gather, a, pr, pc, t):
    most = max(nr, nc)
    dma = pltpu.SemaphoreType.DMA
    b = BAND
    n = a.shape[0]
    heads = (1 + count) * b
    size_r, size_c, size_h, size_g = n // nc, n // nr, heads // nc, b // nc
    outs = [(b, b)] * 6 + [(n, b), (n, b), (heads, b), (n, b), (n, b)]
    if gather:
        outs.append((nc, *t.shape))
    scratch = [
        (n, b), (n, b), (heads, b), (b, b),
        (nc, size_r, b), (nr // 2, size_c, b), (nc, size_h, b), (nr, size_g, b),
        (size_r, b), (size_c, b), (size_h, b), (size_g, b), (nc, size_g, b), (nr, size_h, b), (size_h, b), (n, b),
        (nr // 2, size_c, b), (nr // 2, size_c, b),
    ]
    return pl.pallas_call(
        functools.partial(middle_kernel, nr, nc, first, count, gather),
        out_shape=tuple(jax.ShapeDtypeStruct(s, jnp.float32) for s in outs),
        in_specs=[pl.BlockSpec(memory_space=VMEM)] * 4,
        out_specs=(pl.BlockSpec(memory_space=VMEM),) * len(outs),
        scratch_shapes=[
            *(VMEM(s, jnp.float32) for s in scratch),
            dma((10, most)), dma((10, most)),
            *spread_sems(nc), *spread_sems(nr), *pair_sems(nr), *pair_sems(nr),
        ],
        compiler_params=pltpu.CompilerParams(collective_id=first, has_side_effects=True),
        name=f"middle_{first}",
    )(a, pr, pc, t)


def shards(nr, nc, matrix):
    n = matrix.shape[0]
    b = BAND
    row, col = lax.axis_index("row"), lax.axis_index("col")
    pos = jnp.stack([row, col]).astype(jnp.int32)
    vmem = lambda *shape: VMEM(shape, jnp.float32)
    p1r, p1c, t = spread(nr, nc, matrix)
    *fac, sr, sc, h, er, ec, t = middle(nr, nc, 1, 2, True, matrix, p1r, p1c, t)
    one = call(
        step_one_kernel,
        [(n, n), (n, b), (n, b), (b, b), (b, b)],
        "step_one",
        [vmem(n, 2 * b), vmem(n, 2 * b), vmem(b, 3 * b), vmem(7, b, b)],
    )
    updated, p2r, p2c, t2, a33 = one(pos, *fac, h, t, p1r, sr, er, p1c, sc, ec, matrix)
    *fac, sr, sc, h, er, ec = middle(nr, nc, 2, 1, False, updated, p2r, p2c, t2)
    two = call(
        step_two_kernel,
        [(n, n)],
        "step_two",
        [vmem(n, 2 * b), vmem(n, 2 * b), vmem(b, b), vmem(b, b), vmem(n, n), pltpu.SemaphoreType.DMA((n // b,))],
        pl.ANY,
    )
    return two(pos, *fac, h, a33, p2r, sr, er, p2c, sc, ec, updated)[0]


def solution(mesh):
    spec = P("row", "col")
    body = functools.partial(shards, mesh.shape["row"], mesh.shape["col"])
    return jax.shard_map(body, mesh=mesh, in_specs=(spec,), out_specs=spec, check_vma=False)
```

```python
import functools

import jax
import jax.numpy as jnp
from jax import lax
from jax.experimental import pallas as pl
from jax.experimental.pallas import tpu as pltpu
from jax.sharding import PartitionSpec as P

BAND = 128
HIGH = lax.Precision.HIGHEST
VMEM = pltpu.VMEM
MESH = pl.DeviceIdType.MESH


def dot(left, right):
    return jnp.dot(left, right, precision=HIGH, preferred_element_type=jnp.float32)


def mm(left, right, ca=1, cb=0):
    return lax.dot_general(
        left, right, (((ca,), (cb,)), ((), ())), precision=HIGH, preferred_element_type=jnp.float32
    )


def eliminate(x_ref, jordan):
    n = x_ref.shape[0]
    lane = lax.broadcasted_iota(jnp.int32, (1, n), 1)
    rows = lax.broadcasted_iota(jnp.int32, (n, 1), 0)
    rows8 = lax.broadcasted_iota(jnp.int32, (8, n), 0)
    lane8 = lax.broadcasted_iota(jnp.int32, (8, n), 1)

    def block(j, _):
        at = pl.ds(pl.multiple_of(8 * j, 8), 8)
        full = x_ref[...]
        strip = x_ref[at, :]
        cols = [jnp.broadcast_to(strip[:, i : i + 1], (8, n)) for i in range(8)]
        kept = strip
        for i in range(8):
            if not jordan:
                kept = jnp.where(rows8 == i, strip, kept)
            inv = 1.0 / jnp.broadcast_to(cols[i][i : i + 1, :], (8, n))
            mult = jnp.where(rows8 == i, -inv, cols[i] * inv)
            for k in range(i + 1, 8):
                cols[k] = jnp.where(rows8 == i, 0.0, cols[k]) - mult * cols[k][i : i + 1, :]
            row = jnp.where(lane == i, 1.0, strip[i : i + 1, :])
            strip = jnp.where((rows8 == i) | (lane8 == i), 0.0, strip) - mult * row
        ids = rows - 8 * j
        out = jnp.where(lane < 8, 0.0, full)
        for i in range(8):
            out = out - full[:, i : i + 1] * strip[i : i + 1, :]
        if jordan:
            x_ref[...] = pltpu.roll(out, n - 8, 1)
            x_ref[at, :] = pltpu.roll(strip, n - 8, 1)
        else:
            x_ref[...] = pltpu.roll(jnp.where(ids >= 8, out, full), n - 8, 1)
            x_ref[at, :] = pltpu.roll(kept, n - 8, 1)
        return 0

    lax.fori_loop(0, n // 8, block, 0)


def piece(ref, k):
    parts, _, n = ref.shape
    rows = BAND // parts
    return ref[:, k * rows : (k + 1) * rows, :].reshape(BAND, n)


def whole(ref):
    parts, rows, n = ref.shape
    return ref[...].reshape(parts * rows, n)


def invert_chol(gram, cinv_ref, rinv_ref):
    n = BAND
    r = lax.broadcasted_iota(jnp.int32, (n, n), 0)
    c = lax.broadcasted_iota(jnp.int32, (n, n), 1)
    cinv_ref[...] = gram
    eliminate(cinv_ref, False)
    x = cinv_ref[...]
    diag = jnp.sum(jnp.where(r == c, x, 0.0), axis=1, keepdims=True)
    cinv = jnp.where(r > c, x, (r == c).astype(jnp.float32)) / jnp.sqrt(diag)
    cinv_ref[...] = cinv
    rinv_ref[...] = cinv.T


def invert_top(top, rinv_ref, f_ref, ft_ref, finv_ref, finvt_ref):
    n = BAND
    r = lax.broadcasted_iota(jnp.int32, (n, n), 0)
    c = lax.broadcasted_iota(jnp.int32, (n, n), 1)
    f = dot(top, rinv_ref[...]) + (r == c).astype(jnp.float32)
    f_ref[...] = f
    ft_ref[...] = f.T
    finv_ref[...] = f
    eliminate(finv_ref, True)
    finvt_ref[...] = finv_ref[...].T


def weights(fac, h, s_top, s_topt, a_ss):
    cinv, rinv, _, _, finv, finvt = fac
    half = dot(cinv, h) + s_top
    j = dot(half, rinv) + dot(cinv, s_topt) + a_ss
    return dot(dot(finv, j), finvt)


def step_one_kernel(
    pos_ref, cinv_ref, rinv_ref, f_ref, ft_ref, finv_ref, finvt_ref, h_ref, g_ref,
    pr_ref, sr_ref, er_ref, pc_ref, sc_ref, ec_ref, a_ref,
    updated_ref, p2r_ref, p2c_ref, t2_ref, a33_ref, left_ref, right_ref, ht_ref, small_ref,
):
    b = BAND
    n = pr_ref.shape[0]
    always = pos_ref[0] >= 0
    sums = lambda k: h_ref[k * b : (k + 1) * b, :]
    sumst = lambda k: ht_ref[:, k * b : (k + 1) * b]

    @pl.when(always)
    def _():
        for k in range(3):
            ht_ref[:, k * b : (k + 1) * b] = h_ref[k * b : (k + 1) * b, :].T

    a22, a31, a32, a33, a13, a23 = (functools.partial(piece, g_ref, k) for k in range(1, 7))

    @pl.when(always)
    def _():
        fac = tuple(ref[...] for ref in (cinv_ref, rinv_ref, f_ref, ft_ref, finv_ref, finvt_ref))
        small_ref[0, :, :] = weights(fac, sums(0), sums(1), sumst(1), a22())

    @pl.when(always)
    def _():
        small_ref[6, :, :] = dot(a31(), rinv_ref[...])
        small_ref[3, :, :] = dot(cinv_ref[...], a13())

    def work(slot, house, sums, cols):
        @pl.when(always)
        def _():
            rows = dot(dot(sums, rinv_ref[...]) + cols(), finvt_ref[...])
            small_ref[slot, :, :] = rows - 0.5 * dot(house(), small_ref[0])

    def workt(slot, house, sums, cols):
        @pl.when(always)
        def _():
            rows = dot(finv_ref[...], dot(cinv_ref[...], sums) + cols())
            small_ref[slot, :, :] = rows - 0.5 * dot(small_ref[0], house())

    work(5, lambda: small_ref[6], sums(2), a32)
    work(4, lambda: f_ref[...], sums(1), a22)
    workt(1, lambda: ft_ref[...], sumst(1), a22)
    workt(2, lambda: small_ref[3], sumst(2), a23)

    @pl.when(always)
    def _():
        t2_ref[...] = a32() - dot(small_ref[6], small_ref[1]) - dot(small_ref[5], ft_ref[...])
        a33_ref[...] = a33() - dot(small_ref[6], small_ref[2]) - dot(small_ref[5], small_ref[3])

    tile = 2 * b if n % (2 * b) == 0 else b

    def side(start, p_ref, s_ref, e_ref, out_ref, house_at, work_at, p2_ref):
        @pl.loop(0, n // tile)
        def _(step):
            at = pl.ds(pl.multiple_of(step * tile, tile), tile)
            ids = start * n + step * tile + lax.broadcasted_iota(jnp.int32, (tile, b), 0)
            lane = lax.broadcasted_iota(jnp.int32, (tile, b), 1)
            house = dot(p_ref[at, :], rinv_ref[...]) + (ids - b == lane).astype(jnp.float32)
            cols = e_ref[at, :]
            wk = dot(dot(s_ref[at, :], rinv_ref[...]) + cols, finvt_ref[...]) - 0.5 * dot(house, small_ref[0])
            out_ref[at, house_at : house_at + b] = house
            out_ref[at, work_at : work_at + b] = wk
            p2 = cols - dot(house, small_ref[1]) - dot(wk, ft_ref[...])
            p2_ref[at, :] = jnp.where(ids >= 2 * b, p2, 0.0)

    side(pos_ref[0], pr_ref, sr_ref, er_ref, left_ref, 0, b, p2r_ref)
    side(pos_ref[1], pc_ref, sc_ref, ec_ref, right_ref, b, 0, p2c_ref)

    @pl.loop(0, n // tile)
    def _(step):
        at = pl.ds(pl.multiple_of(step * tile, tile), tile)
        updated_ref[at, :] = a_ref[at, :] - mm(left_ref[at, :], right_ref[...], 1, 1)


def step_two_kernel(
    pos_ref, cinv_ref, rinv_ref, f_ref, ft_ref, finv_ref, finvt_ref, h_ref, a33_ref,
    pr_ref, sr_ref, er_ref, pc_ref, sc_ref, ec_ref, a_ref,
    out_ref, left_ref, right_ref, ht_ref, z_ref, result_ref, sem,
):
    b = BAND
    n = pr_ref.shape[0]
    tile = 2 * b if n % (2 * b) == 0 else b

    @pl.when(pos_ref[0] >= 0)
    def _():
        ht_ref[...] = h_ref[b : 2 * b, :].T

    @pl.when(pos_ref[0] >= 0)
    def _():
        fac = tuple(ref[...] for ref in (cinv_ref, rinv_ref, f_ref, ft_ref, finv_ref, finvt_ref))
        z_ref[...] = weights(fac, h_ref[0:b, :], h_ref[b : 2 * b, :], ht_ref[...], a33_ref[...])

    def side(start, p_ref, s_ref, e_ref, out_ref, house_at, work_at):
        @pl.loop(0, n // tile)
        def _(step):
            at = pl.ds(pl.multiple_of(step * tile, tile), tile)
            ids = start * n + step * tile + lax.broadcasted_iota(jnp.int32, (tile, b), 0)
            lane = lax.broadcasted_iota(jnp.int32, (tile, b), 1)
            house = dot(p_ref[at, :], rinv_ref[...]) + (ids - 2 * b == lane).astype(jnp.float32)
            out_ref[at, house_at : house_at + b] = house
            ay = dot(s_ref[at, :], rinv_ref[...]) + e_ref[at, :]
            out_ref[at, work_at : work_at + b] = dot(ay, finvt_ref[...]) - 0.5 * dot(house, z_ref[...])

    side(pos_ref[0], pr_ref, sr_ref, er_ref, left_ref, 0, b)
    side(pos_ref[1], pc_ref, sc_ref, ec_ref, right_ref, b, 0)

    def store(step):
        at = pl.ds(pl.multiple_of(step * tile, tile), tile)
        return pltpu.make_async_copy(result_ref.at[at], out_ref.at[at], sem.at[step])

    @pl.loop(0, n // tile)
    def _(step):
        at = pl.ds(pl.multiple_of(step * tile, tile), tile)
        result_ref[at, :] = a_ref[at, :] - mm(left_ref[at, :], right_ref[...], 1, 1)
        store(step).start()

    @pl.loop(0, n // tile)
    def _(step):
        store(step).wait()


def call(body, outs, name, scratch, space=VMEM):
    def run(pos, *args):
        return pl.pallas_call(
            body,
            out_shape=tuple(jax.ShapeDtypeStruct(s, jnp.float32) for s in outs),
            in_specs=[pl.BlockSpec(memory_space=pltpu.SMEM)] + [pl.BlockSpec(memory_space=VMEM)] * len(args),
            out_specs=(pl.BlockSpec(memory_space=space),) * len(outs),
            scratch_shapes=scratch,
            name=name,
        )(pos, *args)

    return run


def greet(nr, nc, between=None):
    r, c = lax.axis_index("row"), lax.axis_index("col")
    barrier = pltpu.get_barrier_semaphore()
    for k in range(1, nc):
        pl.semaphore_signal(barrier, inc=1, device_id=(r, (c + k) % nc), device_id_type=MESH)
    for k in range(1, nr):
        pl.semaphore_signal(barrier, inc=1, device_id=((r + k) % nr, c), device_id_type=MESH)
    if between is not None:
        between(r, c)
    pl.semaphore_wait(barrier, nr + nc - 2)
    return r, c


def turn(a, block, out):
    for k in range(a.shape[1] // BAND):
        at = pl.ds(k * BAND, BAND)
        out[at, :] = a[pl.ds(block * BAND, BAND), at].T


def rows_at(index, size):
    return pl.ds(pl.multiple_of(index * size, 8), size)


class Spread:
    def __init__(self, axis, parts, me, other, dst, sems, pair_sems=None):
        self.pair = None if pair_sems is None else PairGather(me, other, parts, dst, pair_sems)
        self.axis, self.parts, self.me, self.other, self.dst = axis, parts, me, other, dst
        self.root_send, self.root_recv, self.send, self.recv = sems
        self.size = dst.shape[0] // parts

    def device(self, k):
        return (self.other, k) if self.axis == "col" else (k, self.other)

    def copy(self, k, src):
        rows = pl.ds(k * self.size, self.size)
        return pltpu.make_async_remote_copy(
            src_ref=src(rows),
            dst_ref=self.dst.at[rows],
            send_sem=self.root_send.at[k],
            recv_sem=self.root_recv,
            device_id=self.device(k),
            device_id_type=MESH,
        )

    def scatter(self, src):
        @pl.when(self.me == 0)
        def _():
            for k in range(1, self.parts):
                self.copy(k, src).start()
            rows = pl.ds(0, self.size)
            self.dst[rows, :] = src(rows)[...]

    def gather(self, src):
        @pl.when(self.me != 0)
        def _():
            self.copy(1, src).wait_recv()

        self.copies = []
        if self.pair is not None:
            self.pair.start()
            return
        for k in range(1, self.parts):
            rows = rows_at(self.me, self.size)
            copy = pltpu.make_async_remote_copy(
                src_ref=self.dst.at[rows],
                dst_ref=self.dst.at[rows],
                send_sem=self.send.at[k],
                recv_sem=self.recv.at[k],
                device_id=self.device((self.me + k) % self.parts),
                device_id_type=MESH,
            )
            copy.start()
            self.copies.append(copy)

    def finish(self, src):
        for copy in self.copies:
            copy.wait()
        if self.pair is not None:
            self.pair.finish()

        @pl.when(self.me == 0)
        def _():
            for k in range(1, self.parts):
                self.copy(k, src).wait_send()


class PairGather:
    def __init__(self, r, c, nr, dst, sems):
        self.r, self.c, self.count, self.dst = r, c, nr // 2, dst
        self.z, self.p = r // 2, r % 2
        self.sems = sems
        self.size = dst.shape[0] // nr

    def copy(self, src, index, to, stage, k):
        return pltpu.make_async_remote_copy(
            src_ref=src,
            dst_ref=self.dst.at[rows_at(index, self.size)],
            send_sem=self.sems[2 * stage].at[k],
            recv_sem=self.sems[2 * stage + 1].at[k],
            device_id=(to, self.c),
            device_id_type=MESH,
        )

    def start(self, src=None):
        src = self.dst.at[rows_at(self.r, self.size)] if src is None else src
        self.partner = 2 * self.z + 1 - self.p
        self.far = []
        for k in range(1, self.count):
            to = 2 * ((self.z + k) % self.count) + self.p
            self.far.append(self.copy(src, self.r, to, 0, k))
        for copy in self.far:
            copy.start()
        self.near = [self.copy(src, self.r, self.partner, 1, 0)]
        self.near[0].start()

    def forward(self):
        for k in sorted(range(1, self.count), key=lambda k: min(k, self.count - k)):
            self.far[k - 1].wait_recv()
            index = 2 * ((self.z + self.count - k) % self.count) + self.p
            copy = self.copy(self.dst.at[rows_at(index, self.size)], index, self.partner, 1, k)
            copy.start()
            self.near.append(copy)

    def finish(self):
        for copy in self.far:
            copy.wait_send()
        for copy in self.near:
            copy.wait()


def pair_sems(nr):
    return [pltpu.SemaphoreType.DMA((nr // 2,)) for _ in range(4)]


def spread_sems(parts):
    dma = pltpu.SemaphoreType.DMA
    return [dma((parts,)), dma, dma((parts,)), dma((parts,))]


def spread_kernel(nr, nc, a, pr, pc, ts, xr, xc, t, *sems):
    rows_sems, cols_sems, (send, recv, down_send, down_recv) = sems[:4], sems[4:8], sems[8:12]
    b = BAND

    def prepare(r, c):
        @pl.when(c == 0)
        def _():
            xr[...] = a[:, 0:b]

        @pl.when(r == 0)
        def _():
            turn(a, 0, xc)

        @pl.when((r == 0) & (c == 0))
        def _():
            xr[0:b, :] = jnp.zeros((b, b), jnp.float32)
            xc[0:b, :] = jnp.zeros((b, b), jnp.float32)
            rows = b // nc
            for k, (i, j) in enumerate(((1, 0), (1, 1), (2, 0), (2, 1), (2, 2), (0, 2), (1, 2))):
                block = a[i * b : (i + 1) * b, j * b : (j + 1) * b]
                t[:, k * rows : (k + 1) * rows, :] = block.reshape(nc, rows, b)

    r, c = greet(nr, nc, prepare)
    rows = Spread("col", nc, c, r, pr, rows_sems)
    cols = Spread("row", nr, r, c, pc, cols_sems, sems[12:])
    rows.scatter(lambda at: xr.at[at])
    cols.scatter(lambda at: xc.at[at])

    def slice_to(k):
        return pltpu.make_async_remote_copy(
            src_ref=t.at[k], dst_ref=ts, send_sem=send.at[k], recv_sem=recv, device_id=(r, k), device_id_type=MESH
        )

    def down(k):
        return pltpu.make_async_remote_copy(
            src_ref=ts, dst_ref=ts, send_sem=down_send.at[k], recv_sem=down_recv, device_id=(k, c), device_id_type=MESH
        )

    @pl.when((r == 0) & (c == 0))
    def _():
        for k in range(1, nc):
            slice_to(k).start()
        ts[...] = t[0]

    rows.gather(lambda at: xr.at[at])
    cols.gather(lambda at: xc.at[at])

    @pl.when((r == 0) & (c != 0))
    def _():
        slice_to(1).wait_recv()

    @pl.when(r == 0)
    def _():
        for k in range(1, nr):
            down(k).start()

    cols.pair.forward()

    @pl.when(r != 0)
    def _():
        down(1).wait_recv()

    rows.finish(lambda at: xr.at[at])
    cols.finish(lambda at: xc.at[at])

    @pl.when(r == 0)
    def _():
        for k in range(1, nr):
            down(k).wait_send()

    @pl.when((r == 0) & (c == 0))
    def _():
        for k in range(1, nc):
            slice_to(k).wait_send()


def middle_kernel(
    nr, nc, first, count, gather, a, pr, pc, t, cinv, rinv, f, ft, finv, finvt, out_r, out_c, out_h, er, ec, *rest
):
    out_t, rest = (rest[0], rest[1:]) if gather else (None, rest)
    sr, sc, h, gram, part_r, part_c, part_h, part_g, sum_r, sum_c, sum_h, sum_g, all_g, cols_h, all_h, xc, part_p, sum_p = rest[:18]
    send, recv, *sems = rest[18:]
    b = BAND
    n = a.shape[0]
    size_r, size_c, size_h, size_g = n // nc, n // nr, h.shape[0] // nc, b // nc

    def prepare(r, c):
        @pl.when(r >= 0)
        def _():
            gram[...] = mm(pr[...], pr[...], 0, 0)
            part_g[r] = gram[rows_at(c, size_g), :]

        @pl.when(r == 0)
        def _():
            turn(a, first, xc)

    r, c = greet(nr, nc, prepare)
    always = r >= 0

    def along(axis, phase, source, target):
        parts, me = (nc, c) if axis == "col" else (nr, r)
        copies = []
        for k in range(1, parts):
            to = (me + k) % parts
            copy = pltpu.make_async_remote_copy(
                src_ref=source(to),
                dst_ref=target(k),
                send_sem=send.at[phase, k],
                recv_sem=recv.at[phase, k],
                device_id=(r, to) if axis == "col" else (to, c),
                device_id_type=MESH,
            )
            copy.start()
            copies.append(copy)
        return copies

    def finish(copies):
        for copy in copies:
            copy.wait()

    def block(body):
        pl.when(always)(body)

    g_copies = along("row", 0, lambda to: gram.at[rows_at(c, size_g)], lambda k: part_g.at[r])
    rows = Spread("col", nc, c, r, er, sems[:4])
    cols = Spread("row", nr, r, c, ec, sems[4:8], sems[8:12])
    gather_c = PairGather(r, c, nr, out_c, sems[12:])
    rows_src = lambda at: a.at[at, first * b : (first + 1) * b]
    cols_src = lambda at: xc.at[at]

    tile = 2 * b if n % (2 * b) == 0 else b

    @pl.loop(0, n // tile)
    def _(step):
        at = pl.ds(pl.multiple_of(step * tile, tile), tile)
        sr[at, :] = dot(a[at, :], pc[...])

    @block
    def _():
        h[0:b, :] = mm(pr[...], sr[...], 0, 0)
        h[b : (1 + count) * b, :] = jnp.where(r == 0, sr[first * b : (first + count) * b, :], 0.0)

    finish(g_copies)
    value = part_g[0]
    for k in range(1, nr):
        value = value + part_g[k]
    sum_g[...] = value
    all_g[c] = value
    g_copies = along("col", 3, lambda to: sum_g, lambda k: all_g.at[c])
    h_copies = along("col", 4, lambda to: h.at[rows_at(to, size_h)], lambda k: part_h.at[k])
    r_copies = along("col", 2, lambda to: sr.at[rows_at(to, size_r)], lambda k: part_r.at[k])
    t_copies = []
    if gather:
        t_copies = along("col", 1, lambda to: t, lambda k: out_t.at[c])
        out_t[c] = t[...]

    @pl.loop(0, n // tile)
    def _(step):
        at = pl.ds(pl.multiple_of(step * tile, tile), tile)
        sc[at, :] = mm(a[:, at], pr[...], 0, 0)

    z, p = r // 2, r % 2
    half = nr // 2
    p_copies = []
    for i in range(half):
        copy = pltpu.make_async_remote_copy(
            src_ref=sc.at[rows_at(2 * i + 1 - p, size_c)],
            dst_ref=part_p.at[i],
            send_sem=send.at[5, i],
            recv_sem=recv.at[5, i],
            device_id=(2 * z + 1 - p, c),
            device_id_type=MESH,
        )
        copy.start()
        p_copies.append(copy)
    rows.scatter(rows_src)
    cols.scatter(cols_src)

    finish(h_copies)
    value = h[rows_at(c, size_h), :]
    for k in range(1, nc):
        value = value + part_h[k]
    sum_h[...] = value
    cols_h[r] = value
    h_copies = along("row", 6, lambda to: sum_h, lambda k: cols_h.at[r])

    finish(p_copies)
    for i in range(half):
        sum_p[i] = sc[rows_at(2 * i + p, size_c), :] + part_p[i]
    c_copies = []
    for k in range(1, half):
        to = (z + k) % half
        copy = pltpu.make_async_remote_copy(
            src_ref=sum_p.at[to],
            dst_ref=part_c.at[k],
            send_sem=send.at[8, k],
            recv_sem=recv.at[8, k],
            device_id=(2 * to + p, c),
            device_id_type=MESH,
        )
        copy.start()
        c_copies.append(copy)

    finish(r_copies)
    value = sr[rows_at(c, size_r), :]
    for k in range(1, nc):
        value = value + part_r[k]
    sum_r[...] = value
    out_r[rows_at(c, size_r), :] = value
    r_copies = along("col", 7, lambda to: sum_r, lambda k: out_r.at[rows_at(c, size_r)])
    finish(g_copies)

    @block
    def _():
        invert_chol(whole(all_g), cinv, rinv)

    finish(h_copies)
    value = cols_h[0]
    for k in range(1, nr):
        value = value + cols_h[k]
    all_h[...] = value
    out_h[rows_at(c, size_h), :] = value
    h_copies = along("col", 9, lambda to: all_h, lambda k: out_h.at[rows_at(c, size_h)])

    finish(c_copies)
    value = sum_p[z]
    for k in range(1, half):
        value = value + part_c[k]
    sum_c[...] = value
    out_c[rows_at(r, size_c), :] = value
    gather_c.start(sum_c)
    rows.gather(rows_src)
    cols.gather(cols_src)
    finish(t_copies)

    @block
    def _():
        invert_top(piece(out_t, 0) if gather else t[...], rinv, f, ft, finv, finvt)

    gather_c.forward()
    cols.pair.forward()
    for copies in (r_copies, h_copies):
        finish(copies)
    gather_c.finish()
    rows.finish(rows_src)
    cols.finish(cols_src)


def spread(nr, nc, a):
    dma = pltpu.SemaphoreType.DMA
    b = BAND
    n = a.shape[0]
    tops = 7 * b // nc
    return pl.pallas_call(
        functools.partial(spread_kernel, nr, nc),
        out_shape=tuple(jax.ShapeDtypeStruct(s, jnp.float32) for s in ((n, b), (n, b), (tops, b))),
        in_specs=[pl.BlockSpec(memory_space=VMEM)],
        out_specs=(pl.BlockSpec(memory_space=VMEM),) * 3,
        scratch_shapes=[
            *(VMEM(s, jnp.float32) for s in ((n, b), (n, b), (nc, tops, b))),
            *spread_sems(nc), *spread_sems(nr), dma((nc,)), dma, dma((nr,)), dma, *pair_sems(nr),
        ],
        compiler_params=pltpu.CompilerParams(collective_id=0, has_side_effects=True),
        name="spread",
    )(a)


def middle(nr, nc, first, count, gather, a, pr, pc, t):
    most = max(nr, nc)
    dma = pltpu.SemaphoreType.DMA
    b = BAND
    n = a.shape[0]
    heads = (1 + count) * b
    size_r, size_c, size_h, size_g = n // nc, n // nr, heads // nc, b // nc
    outs = [(b, b)] * 6 + [(n, b), (n, b), (heads, b), (n, b), (n, b)]
    if gather:
        outs.append((nc, *t.shape))
    scratch = [
        (n, b), (n, b), (heads, b), (b, b),
        (nc, size_r, b), (nr // 2, size_c, b), (nc, size_h, b), (nr, size_g, b),
        (size_r, b), (size_c, b), (size_h, b), (size_g, b), (nc, size_g, b), (nr, size_h, b), (size_h, b), (n, b),
        (nr // 2, size_c, b), (nr // 2, size_c, b),
    ]
    return pl.pallas_call(
        functools.partial(middle_kernel, nr, nc, first, count, gather),
        out_shape=tuple(jax.ShapeDtypeStruct(s, jnp.float32) for s in outs),
        in_specs=[pl.BlockSpec(memory_space=VMEM)] * 4,
        out_specs=(pl.BlockSpec(memory_space=VMEM),) * len(outs),
        scratch_shapes=[
            *(VMEM(s, jnp.float32) for s in scratch),
            dma((10, most)), dma((10, most)),
            *spread_sems(nc), *spread_sems(nr), *pair_sems(nr), *pair_sems(nr),
        ],
        compiler_params=pltpu.CompilerParams(collective_id=first, has_side_effects=True),
        name=f"middle_{first}",
    )(a, pr, pc, t)


def shards(nr, nc, matrix):
    n = matrix.shape[0]
    b = BAND
    row, col = lax.axis_index("row"), lax.axis_index("col")
    pos = jnp.stack([row, col]).astype(jnp.int32)
    vmem = lambda *shape: VMEM(shape, jnp.float32)
    p1r, p1c, t = spread(nr, nc, matrix)
    *fac, sr, sc, h, er, ec, t = middle(nr, nc, 1, 2, True, matrix, p1r, p1c, t)
    one = call(
        step_one_kernel,
        [(n, n), (n, b), (n, b), (b, b), (b, b)],
        "step_one",
        [vmem(n, 2 * b), vmem(n, 2 * b), vmem(b, 3 * b), vmem(7, b, b)],
    )
    updated, p2r, p2c, t2, a33 = one(pos, *fac, h, t, p1r, sr, er, p1c, sc, ec, matrix)
    *fac, sr, sc, h, er, ec = middle(nr, nc, 2, 1, False, updated, p2r, p2c, t2)
    two = call(
        step_two_kernel,
        [(n, n)],
        "step_two",
        [vmem(n, 2 * b), vmem(n, 2 * b), vmem(b, b), vmem(b, b), vmem(n, n), pltpu.SemaphoreType.DMA((n // b,))],
        pl.ANY,
    )
    return two(pos, *fac, h, a33, p2r, sr, er, p2c, sc, ec, updated)[0]


def solution(mesh):
    spec = P("row", "col")
    body = functools.partial(shards, mesh.shape["row"], mesh.shape["col"])
    return jax.shard_map(body, mesh=mesh, in_specs=(spec,), out_specs=spec, check_vma=False)
```

```python
import functools

import jax
import jax.numpy as jnp
from jax import lax
from jax.experimental import pallas as pl
from jax.experimental.pallas import tpu as pltpu
from jax.sharding import PartitionSpec as P

BAND = 128
HIGH = lax.Precision.HIGHEST
VMEM = pltpu.VMEM
MESH = pl.DeviceIdType.MESH


def dot(left, right):
    return jnp.dot(left, right, precision=HIGH, preferred_element_type=jnp.float32)


def mm(left, right, ca=1, cb=0):
    return lax.dot_general(
        left, right, (((ca,), (cb,)), ((), ())), precision=HIGH, preferred_element_type=jnp.float32
    )


def outer(left, right):
    def parts(x):
        hi = x.astype(jnp.bfloat16)
        return hi, (x - hi.astype(jnp.float32)).astype(jnp.bfloat16)

    def product(x, y):
        return lax.dot_general(x, y, (((1,), (1,)), ((), ())), preferred_element_type=jnp.float32)

    (lh, ll), (rh, rl) = parts(left), parts(right)
    return product(lh, rh) + (product(lh, rl) + product(ll, rh))


def eliminate(x_ref, jordan):
    n = x_ref.shape[0]
    lane = lax.broadcasted_iota(jnp.int32, (1, n), 1)
    rows = lax.broadcasted_iota(jnp.int32, (n, 1), 0)
    rows8 = lax.broadcasted_iota(jnp.int32, (8, n), 0)
    lane8 = lax.broadcasted_iota(jnp.int32, (8, n), 1)

    def block(j, _):
        at = pl.ds(pl.multiple_of(8 * j, 8), 8)
        full = x_ref[...]
        strip = x_ref[at, :]
        cols = [jnp.broadcast_to(strip[:, i : i + 1], (8, n)) for i in range(8)]
        kept = strip
        for i in range(8):
            if not jordan:
                kept = jnp.where(rows8 == i, strip, kept)
            inv = 1.0 / jnp.broadcast_to(cols[i][i : i + 1, :], (8, n))
            mult = jnp.where(rows8 == i, -inv, cols[i] * inv)
            for k in range(i + 1, 8):
                cols[k] = jnp.where(rows8 == i, 0.0, cols[k]) - mult * cols[k][i : i + 1, :]
            row = jnp.where(lane == i, 1.0, strip[i : i + 1, :])
            strip = jnp.where((rows8 == i) | (lane8 == i), 0.0, strip) - mult * row
        ids = rows - 8 * j
        out = jnp.where(lane < 8, 0.0, full)
        for i in range(8):
            out = out - full[:, i : i + 1] * strip[i : i + 1, :]
        if jordan:
            x_ref[...] = pltpu.roll(out, n - 8, 1)
            x_ref[at, :] = pltpu.roll(strip, n - 8, 1)
        else:
            x_ref[...] = pltpu.roll(jnp.where(ids >= 8, out, full), n - 8, 1)
            x_ref[at, :] = pltpu.roll(kept, n - 8, 1)
        return 0

    lax.fori_loop(0, n // 8, block, 0)


def piece(ref, k):
    parts, _, n = ref.shape
    rows = BAND // parts
    return ref[:, k * rows : (k + 1) * rows, :].reshape(BAND, n)


def whole(ref):
    parts, rows, n = ref.shape
    return ref[...].reshape(parts * rows, n)


def invert_chol(gram, cinv_ref, rinv_ref):
    n = BAND
    r = lax.broadcasted_iota(jnp.int32, (n, n), 0)
    c = lax.broadcasted_iota(jnp.int32, (n, n), 1)
    cinv_ref[...] = gram
    eliminate(cinv_ref, False)
    x = cinv_ref[...]
    diag = jnp.sum(jnp.where(r == c, x, 0.0), axis=1, keepdims=True)
    cinv = jnp.where(r > c, x, (r == c).astype(jnp.float32)) / jnp.sqrt(diag)
    cinv_ref[...] = cinv
    rinv_ref[...] = cinv.T


def invert_top(top, rinv_ref, f_ref, ft_ref, finv_ref, finvt_ref):
    n = BAND
    r = lax.broadcasted_iota(jnp.int32, (n, n), 0)
    c = lax.broadcasted_iota(jnp.int32, (n, n), 1)
    f = dot(top, rinv_ref[...]) + (r == c).astype(jnp.float32)
    f_ref[...] = f
    ft_ref[...] = f.T
    finv_ref[...] = f
    eliminate(finv_ref, True)
    finvt_ref[...] = finv_ref[...].T


def weights(fac, h, s_top, s_topt, a_ss):
    cinv, rinv, _, _, finv, finvt = fac
    half = dot(cinv, h) + s_top
    j = dot(half, rinv) + dot(cinv, s_topt) + a_ss
    return dot(dot(finv, j), finvt)


def step_one_kernel(
    pos_ref, cinv_ref, rinv_ref, f_ref, ft_ref, finv_ref, finvt_ref, h_ref, g_ref,
    pr_ref, sr_ref, er_ref, pc_ref, sc_ref, ec_ref, a_ref,
    updated_ref, p2r_ref, p2c_ref, t2_ref, a33_ref, left_ref, right_ref, ht_ref, zw_ref, small_ref,
):
    b = BAND
    n = pr_ref.shape[0]
    always = pos_ref[0] >= 0
    sums = lambda k: h_ref[k * b : (k + 1) * b, :]
    sumst = lambda k: ht_ref[:, k * b : (k + 1) * b]

    @pl.when(always)
    def _():
        for k in range(3):
            ht_ref[:, k * b : (k + 1) * b] = h_ref[k * b : (k + 1) * b, :].T

    a22, a31, a32, a33, a13, a23 = (functools.partial(piece, g_ref, k) for k in range(1, 7))

    @pl.when(always)
    def _():
        fac = tuple(ref[...] for ref in (cinv_ref, rinv_ref, f_ref, ft_ref, finv_ref, finvt_ref))
        small_ref[0, :, :] = weights(fac, sums(0), sums(1), sumst(1), a22())

    @pl.when(always)
    def _():
        small_ref[6, :, :] = dot(a31(), rinv_ref[...])
        small_ref[3, :, :] = dot(cinv_ref[...], a13())

    def work(slot, house, sums, cols):
        @pl.when(always)
        def _():
            rows = dot(dot(sums, rinv_ref[...]) + cols(), finvt_ref[...])
            small_ref[slot, :, :] = rows - 0.5 * dot(house(), small_ref[0])

    def workt(slot, house, sums, cols):
        @pl.when(always)
        def _():
            rows = dot(finv_ref[...], dot(cinv_ref[...], sums) + cols())
            small_ref[slot, :, :] = rows - 0.5 * dot(small_ref[0], house())

    work(5, lambda: small_ref[6], sums(2), a32)
    work(4, lambda: f_ref[...], sums(1), a22)
    workt(1, lambda: ft_ref[...], sumst(1), a22)
    workt(2, lambda: small_ref[3], sumst(2), a23)

    @pl.when(always)
    def _():
        zw_ref[:, 0:b] = small_ref[0]
        zw_ref[:, b : 2 * b] = small_ref[1]
        t2_ref[...] = a32() - dot(small_ref[6], small_ref[1]) - dot(small_ref[5], ft_ref[...])
        a33_ref[...] = a33() - dot(small_ref[6], small_ref[2]) - dot(small_ref[5], small_ref[3])

    tile = 2 * b if n % (2 * b) == 0 else b

    def side(start, p_ref, s_ref, e_ref, out_ref, house_at, work_at, p2_ref):
        @pl.loop(0, n // tile)
        def _(step):
            at = pl.ds(pl.multiple_of(step * tile, tile), tile)
            ids = start * n + step * tile + lax.broadcasted_iota(jnp.int32, (tile, b), 0)
            lane = lax.broadcasted_iota(jnp.int32, (tile, b), 1)
            house = dot(p_ref[at, :], rinv_ref[...]) + (ids - b == lane).astype(jnp.float32)
            cols = e_ref[at, :]
            both = dot(house, zw_ref[...])
            wk = dot(dot(s_ref[at, :], rinv_ref[...]) + cols, finvt_ref[...]) - 0.5 * both[:, :b]
            out_ref[at, house_at : house_at + b] = house
            out_ref[at, work_at : work_at + b] = wk
            p2 = cols - both[:, b:] - dot(wk, ft_ref[...])
            p2_ref[at, :] = jnp.where(ids >= 2 * b, p2, 0.0)

    side(pos_ref[0], pr_ref, sr_ref, er_ref, left_ref, 0, b, p2r_ref)
    side(pos_ref[1], pc_ref, sc_ref, ec_ref, right_ref, b, 0, p2c_ref)

    @pl.loop(0, n // tile)
    def _(step):
        at = pl.ds(pl.multiple_of(step * tile, tile), tile)
        updated_ref[at, :] = a_ref[at, :] - outer(left_ref[at, :], right_ref[...])


def step_two_kernel(
    pos_ref, cinv_ref, rinv_ref, f_ref, ft_ref, finv_ref, finvt_ref, h_ref, a33_ref,
    pr_ref, sr_ref, er_ref, pc_ref, sc_ref, ec_ref, a_ref,
    out_ref, left_ref, right_ref, ht_ref, z_ref, result_ref, sem,
):
    b = BAND
    n = pr_ref.shape[0]
    tile = 2 * b if n % (2 * b) == 0 else b

    @pl.when(pos_ref[0] >= 0)
    def _():
        ht_ref[...] = h_ref[b : 2 * b, :].T

    @pl.when(pos_ref[0] >= 0)
    def _():
        fac = tuple(ref[...] for ref in (cinv_ref, rinv_ref, f_ref, ft_ref, finv_ref, finvt_ref))
        z_ref[...] = weights(fac, h_ref[0:b, :], h_ref[b : 2 * b, :], ht_ref[...], a33_ref[...])

    def side(start, p_ref, s_ref, e_ref, out_ref, house_at, work_at):
        @pl.loop(0, n // tile)
        def _(step):
            at = pl.ds(pl.multiple_of(step * tile, tile), tile)
            ids = start * n + step * tile + lax.broadcasted_iota(jnp.int32, (tile, b), 0)
            lane = lax.broadcasted_iota(jnp.int32, (tile, b), 1)
            house = dot(p_ref[at, :], rinv_ref[...]) + (ids - 2 * b == lane).astype(jnp.float32)
            out_ref[at, house_at : house_at + b] = house
            ay = dot(s_ref[at, :], rinv_ref[...]) + e_ref[at, :]
            out_ref[at, work_at : work_at + b] = dot(ay, finvt_ref[...]) - 0.5 * dot(house, z_ref[...])

    side(pos_ref[0], pr_ref, sr_ref, er_ref, left_ref, 0, b)
    side(pos_ref[1], pc_ref, sc_ref, ec_ref, right_ref, b, 0)

    def store(step):
        at = pl.ds(pl.multiple_of(step * tile, tile), tile)
        return pltpu.make_async_copy(result_ref.at[at], out_ref.at[at], sem.at[step])

    @pl.loop(0, n // tile)
    def _(step):
        at = pl.ds(pl.multiple_of(step * tile, tile), tile)
        result_ref[at, :] = a_ref[at, :] - outer(left_ref[at, :], right_ref[...])
        store(step).start()

    @pl.loop(0, n // tile)
    def _(step):
        store(step).wait()


def call(body, outs, name, scratch, space=VMEM):
    def run(pos, *args):
        return pl.pallas_call(
            body,
            out_shape=tuple(jax.ShapeDtypeStruct(s, jnp.float32) for s in outs),
            in_specs=[pl.BlockSpec(memory_space=pltpu.SMEM)] + [pl.BlockSpec(memory_space=VMEM)] * len(args),
            out_specs=(pl.BlockSpec(memory_space=space),) * len(outs),
            scratch_shapes=scratch,
            name=name,
        )(pos, *args)

    return run


def greet(nr, nc, between=None):
    r, c = lax.axis_index("row"), lax.axis_index("col")
    barrier = pltpu.get_barrier_semaphore()
    for k in range(1, nc):
        pl.semaphore_signal(barrier, inc=1, device_id=(r, (c + k) % nc), device_id_type=MESH)
    for k in range(1, nr):
        pl.semaphore_signal(barrier, inc=1, device_id=((r + k) % nr, c), device_id_type=MESH)
    if between is not None:
        between(r, c)
    pl.semaphore_wait(barrier, nr + nc - 2)
    return r, c


def turn(a, block, out):
    for k in range(a.shape[1] // BAND):
        at = pl.ds(k * BAND, BAND)
        out[at, :] = a[pl.ds(block * BAND, BAND), at].T


def rows_at(index, size):
    return pl.ds(pl.multiple_of(index * size, 8), size)


class Spread:
    def __init__(self, axis, parts, me, other, dst, sems, pair_sems=None):
        self.pair = None if pair_sems is None else PairGather(me, other, parts, dst, pair_sems)
        self.axis, self.parts, self.me, self.other, self.dst = axis, parts, me, other, dst
        self.root_send, self.root_recv, self.send, self.recv = sems
        self.size = dst.shape[0] // parts

    def device(self, k):
        return (self.other, k) if self.axis == "col" else (k, self.other)

    def copy(self, k, src):
        rows = pl.ds(k * self.size, self.size)
        return pltpu.make_async_remote_copy(
            src_ref=src(rows),
            dst_ref=self.dst.at[rows],
            send_sem=self.root_send.at[k],
            recv_sem=self.root_recv,
            device_id=self.device(k),
            device_id_type=MESH,
        )

    def scatter(self, src):
        @pl.when(self.me == 0)
        def _():
            for k in range(1, self.parts):
                self.copy(k, src).start()
            rows = pl.ds(0, self.size)
            self.dst[rows, :] = src(rows)[...]

    def gather(self, src):
        @pl.when(self.me != 0)
        def _():
            self.copy(1, src).wait_recv()

        self.copies = []
        if self.pair is not None:
            self.pair.start()
            return
        for k in range(1, self.parts):
            rows = rows_at(self.me, self.size)
            copy = pltpu.make_async_remote_copy(
                src_ref=self.dst.at[rows],
                dst_ref=self.dst.at[rows],
                send_sem=self.send.at[k],
                recv_sem=self.recv.at[k],
                device_id=self.device((self.me + k) % self.parts),
                device_id_type=MESH,
            )
            copy.start()
            self.copies.append(copy)

    def finish(self, src):
        for copy in self.copies:
            copy.wait()
        if self.pair is not None:
            self.pair.finish()

        @pl.when(self.me == 0)
        def _():
            for k in range(1, self.parts):
                self.copy(k, src).wait_send()


class PairGather:
    def __init__(self, r, c, nr, dst, sems):
        self.r, self.c, self.count, self.dst = r, c, nr // 2, dst
        self.z, self.p = r // 2, r % 2
        self.sems = sems
        self.size = dst.shape[0] // nr

    def copy(self, src, index, to, stage, k):
        return pltpu.make_async_remote_copy(
            src_ref=src,
            dst_ref=self.dst.at[rows_at(index, self.size)],
            send_sem=self.sems[2 * stage].at[k],
            recv_sem=self.sems[2 * stage + 1].at[k],
            device_id=(to, self.c),
            device_id_type=MESH,
        )

    def start(self, src=None):
        src = self.dst.at[rows_at(self.r, self.size)] if src is None else src
        self.partner = 2 * self.z + 1 - self.p
        self.far = []
        for k in range(1, self.count):
            to = 2 * ((self.z + k) % self.count) + self.p
            self.far.append(self.copy(src, self.r, to, 0, k))
        for copy in self.far:
            copy.start()
        self.near = [self.copy(src, self.r, self.partner, 1, 0)]
        self.near[0].start()

    def forward(self):
        for k in sorted(range(1, self.count), key=lambda k: min(k, self.count - k)):
            self.far[k - 1].wait_recv()
            index = 2 * ((self.z + self.count - k) % self.count) + self.p
            copy = self.copy(self.dst.at[rows_at(index, self.size)], index, self.partner, 1, k)
            copy.start()
            self.near.append(copy)

    def finish(self):
        for copy in self.far:
            copy.wait_send()
        for copy in self.near:
            copy.wait()


def pair_sems(nr):
    return [pltpu.SemaphoreType.DMA((nr // 2,)) for _ in range(4)]


def spread_sems(parts):
    dma = pltpu.SemaphoreType.DMA
    return [dma((parts,)), dma, dma((parts,)), dma((parts,))]


def spread_kernel(nr, nc, a, pr, pc, ts, xr, xc, t, *sems):
    rows_sems, cols_sems, (send, recv, down_send, down_recv) = sems[:4], sems[4:8], sems[8:12]
    b = BAND

    def prepare(r, c):
        @pl.when(c == 0)
        def _():
            xr[...] = a[:, 0:b]

        @pl.when(r == 0)
        def _():
            turn(a, 0, xc)

        @pl.when((r == 0) & (c == 0))
        def _():
            xr[0:b, :] = jnp.zeros((b, b), jnp.float32)
            xc[0:b, :] = jnp.zeros((b, b), jnp.float32)
            rows = b // nc
            for k, (i, j) in enumerate(((1, 0), (1, 1), (2, 0), (2, 1), (2, 2), (0, 2), (1, 2))):
                block = a[i * b : (i + 1) * b, j * b : (j + 1) * b]
                t[:, k * rows : (k + 1) * rows, :] = block.reshape(nc, rows, b)

    r, c = greet(nr, nc, prepare)
    rows = Spread("col", nc, c, r, pr, rows_sems)
    cols = Spread("row", nr, r, c, pc, cols_sems, sems[12:])
    rows.scatter(lambda at: xr.at[at])
    cols.scatter(lambda at: xc.at[at])

    def slice_to(k):
        return pltpu.make_async_remote_copy(
            src_ref=t.at[k], dst_ref=ts, send_sem=send.at[k], recv_sem=recv, device_id=(r, k), device_id_type=MESH
        )

    def down(k):
        return pltpu.make_async_remote_copy(
            src_ref=ts, dst_ref=ts, send_sem=down_send.at[k], recv_sem=down_recv, device_id=(k, c), device_id_type=MESH
        )

    @pl.when((r == 0) & (c == 0))
    def _():
        for k in range(1, nc):
            slice_to(k).start()
        ts[...] = t[0]

    rows.gather(lambda at: xr.at[at])
    cols.gather(lambda at: xc.at[at])

    @pl.when((r == 0) & (c != 0))
    def _():
        slice_to(1).wait_recv()

    @pl.when(r == 0)
    def _():
        for k in range(1, nr):
            down(k).start()

    cols.pair.forward()

    @pl.when(r != 0)
    def _():
        down(1).wait_recv()

    rows.finish(lambda at: xr.at[at])
    cols.finish(lambda at: xc.at[at])

    @pl.when(r == 0)
    def _():
        for k in range(1, nr):
            down(k).wait_send()

    @pl.when((r == 0) & (c == 0))
    def _():
        for k in range(1, nc):
            slice_to(k).wait_send()


def middle_kernel(
    nr, nc, first, count, gather, a, pr, pc, t, cinv, rinv, f, ft, finv, finvt, out_r, out_c, out_h, er, ec, *rest
):
    out_t, rest = (rest[0], rest[1:]) if gather else (None, rest)
    sr, sc, h, gram, part_r, part_c, part_h, part_g, sum_r, sum_c, sum_h, sum_g, all_g, cols_h, all_h, xc, part_p, sum_p = rest[:18]
    send, recv, *sems = rest[18:]
    b = BAND
    n = a.shape[0]
    size_r, size_c, size_h, size_g = n // nc, n // nr, h.shape[0] // nc, b // nc

    def prepare(r, c):
        @pl.when(r >= 0)
        def _():
            gram[...] = mm(pr[...], pr[...], 0, 0)
            part_g[r] = gram[rows_at(c, size_g), :]

        @pl.when(r == 0)
        def _():
            turn(a, first, xc)

    r, c = greet(nr, nc, prepare)
    always = r >= 0

    def along(axis, phase, source, target):
        parts, me = (nc, c) if axis == "col" else (nr, r)
        copies = []
        for k in range(1, parts):
            to = (me + k) % parts
            copy = pltpu.make_async_remote_copy(
                src_ref=source(to),
                dst_ref=target(k),
                send_sem=send.at[phase, k],
                recv_sem=recv.at[phase, k],
                device_id=(r, to) if axis == "col" else (to, c),
                device_id_type=MESH,
            )
            copy.start()
            copies.append(copy)
        return copies

    def finish(copies):
        for copy in copies:
            copy.wait()

    def block(body):
        pl.when(always)(body)

    g_copies = along("row", 0, lambda to: gram.at[rows_at(c, size_g)], lambda k: part_g.at[r])
    rows = Spread("col", nc, c, r, er, sems[:4])
    cols = Spread("row", nr, r, c, ec, sems[4:8], sems[8:12])
    gather_c = PairGather(r, c, nr, out_c, sems[12:])
    rows_src = lambda at: a.at[at, first * b : (first + 1) * b]
    cols_src = lambda at: xc.at[at]
    rows.scatter(rows_src)
    cols.scatter(cols_src)

    tile = 2 * b if n % (2 * b) == 0 else b

    @pl.loop(0, n // tile)
    def _(step):
        at = pl.ds(pl.multiple_of(step * tile, tile), tile)
        sr[at, :] = dot(a[at, :], pc[...])

    @block
    def _():
        h[0:b, :] = mm(pr[...], sr[...], 0, 0)
        h[b : (1 + count) * b, :] = jnp.where(r == 0, sr[first * b : (first + count) * b, :], 0.0)

    finish(g_copies)
    value = part_g[0]
    for k in range(1, nr):
        value = value + part_g[k]
    sum_g[...] = value
    all_g[c] = value
    g_copies = along("col", 3, lambda to: sum_g, lambda k: all_g.at[c])
    h_copies = along("col", 4, lambda to: h.at[rows_at(to, size_h)], lambda k: part_h.at[k])
    r_copies = along("col", 2, lambda to: sr.at[rows_at(to, size_r)], lambda k: part_r.at[k])
    t_copies = []
    if gather:
        t_copies = along("col", 1, lambda to: t, lambda k: out_t.at[c])
        out_t[c] = t[...]

    @pl.loop(0, n // tile)
    def _(step):
        at = pl.ds(pl.multiple_of(step * tile, tile), tile)
        sc[at, :] = mm(a[:, at], pr[...], 0, 0)

    z, p = r // 2, r % 2
    half = nr // 2
    p_copies = []
    for i in range(half):
        copy = pltpu.make_async_remote_copy(
            src_ref=sc.at[rows_at(2 * i + 1 - p, size_c)],
            dst_ref=part_p.at[i],
            send_sem=send.at[5, i],
            recv_sem=recv.at[5, i],
            device_id=(2 * z + 1 - p, c),
            device_id_type=MESH,
        )
        copy.start()
        p_copies.append(copy)

    finish(h_copies)
    value = h[rows_at(c, size_h), :]
    for k in range(1, nc):
        value = value + part_h[k]
    sum_h[...] = value
    cols_h[r] = value
    h_copies = along("row", 6, lambda to: sum_h, lambda k: cols_h.at[r])

    finish(p_copies)
    for i in range(half):
        sum_p[i] = sc[rows_at(2 * i + p, size_c), :] + part_p[i]
    c_copies = []
    for k in range(1, half):
        to = (z + k) % half
        copy = pltpu.make_async_remote_copy(
            src_ref=sum_p.at[to],
            dst_ref=part_c.at[k],
            send_sem=send.at[8, k],
            recv_sem=recv.at[8, k],
            device_id=(2 * to + p, c),
            device_id_type=MESH,
        )
        copy.start()
        c_copies.append(copy)

    finish(r_copies)
    value = sr[rows_at(c, size_r), :]
    for k in range(1, nc):
        value = value + part_r[k]
    sum_r[...] = value
    out_r[rows_at(c, size_r), :] = value
    r_copies = along("col", 7, lambda to: sum_r, lambda k: out_r.at[rows_at(c, size_r)])
    rows.gather(rows_src)
    cols.gather(cols_src)
    finish(g_copies)

    @block
    def _():
        invert_chol(whole(all_g), cinv, rinv)

    finish(h_copies)
    value = cols_h[0]
    for k in range(1, nr):
        value = value + cols_h[k]
    all_h[...] = value
    out_h[rows_at(c, size_h), :] = value
    h_copies = along("col", 9, lambda to: all_h, lambda k: out_h.at[rows_at(c, size_h)])

    finish(c_copies)
    value = sum_p[z]
    for k in range(1, half):
        value = value + part_c[k]
    sum_c[...] = value
    out_c[rows_at(r, size_c), :] = value
    gather_c.start(sum_c)
    finish(t_copies)

    @block
    def _():
        invert_top(piece(out_t, 0) if gather else t[...], rinv, f, ft, finv, finvt)

    gather_c.forward()
    cols.pair.forward()
    for copies in (r_copies, h_copies):
        finish(copies)
    gather_c.finish()
    rows.finish(rows_src)
    cols.finish(cols_src)


def spread(nr, nc, a):
    dma = pltpu.SemaphoreType.DMA
    b = BAND
    n = a.shape[0]
    tops = 7 * b // nc
    return pl.pallas_call(
        functools.partial(spread_kernel, nr, nc),
        out_shape=tuple(jax.ShapeDtypeStruct(s, jnp.float32) for s in ((n, b), (n, b), (tops, b))),
        in_specs=[pl.BlockSpec(memory_space=VMEM)],
        out_specs=(pl.BlockSpec(memory_space=VMEM),) * 3,
        scratch_shapes=[
            *(VMEM(s, jnp.float32) for s in ((n, b), (n, b), (nc, tops, b))),
            *spread_sems(nc), *spread_sems(nr), dma((nc,)), dma, dma((nr,)), dma, *pair_sems(nr),
        ],
        compiler_params=pltpu.CompilerParams(collective_id=0, has_side_effects=True),
        name="spread",
    )(a)


def middle(nr, nc, first, count, gather, a, pr, pc, t):
    most = max(nr, nc)
    dma = pltpu.SemaphoreType.DMA
    b = BAND
    n = a.shape[0]
    heads = (1 + count) * b
    size_r, size_c, size_h, size_g = n // nc, n // nr, heads // nc, b // nc
    outs = [(b, b)] * 6 + [(n, b), (n, b), (heads, b), (n, b), (n, b)]
    if gather:
        outs.append((nc, *t.shape))
    scratch = [
        (n, b), (n, b), (heads, b), (b, b),
        (nc, size_r, b), (nr // 2, size_c, b), (nc, size_h, b), (nr, size_g, b),
        (size_r, b), (size_c, b), (size_h, b), (size_g, b), (nc, size_g, b), (nr, size_h, b), (size_h, b), (n, b),
        (nr // 2, size_c, b), (nr // 2, size_c, b),
    ]
    return pl.pallas_call(
        functools.partial(middle_kernel, nr, nc, first, count, gather),
        out_shape=tuple(jax.ShapeDtypeStruct(s, jnp.float32) for s in outs),
        in_specs=[pl.BlockSpec(memory_space=VMEM)] * 4,
        out_specs=(pl.BlockSpec(memory_space=VMEM),) * len(outs),
        scratch_shapes=[
            *(VMEM(s, jnp.float32) for s in scratch),
            dma((10, most)), dma((10, most)),
            *spread_sems(nc), *spread_sems(nr), *pair_sems(nr), *pair_sems(nr),
        ],
        compiler_params=pltpu.CompilerParams(collective_id=first, has_side_effects=True),
        name=f"middle_{first}",
    )(a, pr, pc, t)


def shards(nr, nc, matrix):
    n = matrix.shape[0]
    b = BAND
    row, col = lax.axis_index("row"), lax.axis_index("col")
    pos = jnp.stack([row, col]).astype(jnp.int32)
    vmem = lambda *shape: VMEM(shape, jnp.float32)
    p1r, p1c, t = spread(nr, nc, matrix)
    *fac, sr, sc, h, er, ec, t = middle(nr, nc, 1, 2, True, matrix, p1r, p1c, t)
    one = call(
        step_one_kernel,
        [(n, n), (n, b), (n, b), (b, b), (b, b)],
        "step_one",
        [vmem(n, 2 * b), vmem(n, 2 * b), vmem(b, 3 * b), vmem(b, 2 * b), vmem(7, b, b)],
    )
    updated, p2r, p2c, t2, a33 = one(pos, *fac, h, t, p1r, sr, er, p1c, sc, ec, matrix)
    *fac, sr, sc, h, er, ec = middle(nr, nc, 2, 1, False, updated, p2r, p2c, t2)
    two = call(
        step_two_kernel,
        [(n, n)],
        "step_two",
        [vmem(n, 2 * b), vmem(n, 2 * b), vmem(b, b), vmem(b, b), vmem(n, n), pltpu.SemaphoreType.DMA((n // b,))],
        pl.ANY,
    )
    return two(pos, *fac, h, a33, p2r, sr, er, p2c, sc, ec, updated)[0]


def solution(mesh):
    spec = P("row", "col")
    body = functools.partial(shards, mesh.shape["row"], mesh.shape["col"])
    return jax.shard_map(body, mesh=mesh, in_specs=(spec,), out_specs=spec, check_vma=False)
```

```python
import functools

import jax
import jax.numpy as jnp
from jax import lax
from jax.experimental import pallas as pl
from jax.experimental.pallas import tpu as pltpu
from jax.sharding import PartitionSpec as P

BAND = 128
HIGH = lax.Precision.HIGHEST
VMEM = pltpu.VMEM
MESH = pl.DeviceIdType.MESH


def dot(left, right):
    return jnp.dot(left, right, precision=HIGH, preferred_element_type=jnp.float32)


def mm(left, right, ca=1, cb=0):
    return lax.dot_general(
        left, right, (((ca,), (cb,)), ((), ())), precision=HIGH, preferred_element_type=jnp.float32
    )


def outer(left, right):
    def parts(x):
        hi = x.astype(jnp.bfloat16)
        return hi, (x - hi.astype(jnp.float32)).astype(jnp.bfloat16)

    def product(x, y):
        return lax.dot_general(x, y, (((1,), (1,)), ((), ())), preferred_element_type=jnp.float32)

    (lh, ll), (rh, rl) = parts(left), parts(right)
    return product(lh, rh) + (product(lh, rl) + product(ll, rh))


def eliminate(x_ref, jordan):
    n = x_ref.shape[0]
    lane = lax.broadcasted_iota(jnp.int32, (1, n), 1)
    rows = lax.broadcasted_iota(jnp.int32, (n, 1), 0)
    rows8 = lax.broadcasted_iota(jnp.int32, (8, n), 0)
    lane8 = lax.broadcasted_iota(jnp.int32, (8, n), 1)

    def block(j, _):
        at = pl.ds(pl.multiple_of(8 * j, 8), 8)
        full = x_ref[...]
        strip = x_ref[at, :]
        cols = [jnp.broadcast_to(strip[:, i : i + 1], (8, n)) for i in range(8)]
        kept = strip
        for i in range(8):
            if not jordan:
                kept = jnp.where(rows8 == i, strip, kept)
            inv = 1.0 / jnp.broadcast_to(cols[i][i : i + 1, :], (8, n))
            mult = jnp.where(rows8 == i, -inv, cols[i] * inv)
            for k in range(i + 1, 8):
                cols[k] = jnp.where(rows8 == i, 0.0, cols[k]) - mult * cols[k][i : i + 1, :]
            row = jnp.where(lane == i, 1.0, strip[i : i + 1, :])
            strip = jnp.where((rows8 == i) | (lane8 == i), 0.0, strip) - mult * row
        ids = rows - 8 * j
        out = jnp.where(lane < 8, 0.0, full)
        for i in range(8):
            out = out - full[:, i : i + 1] * strip[i : i + 1, :]
        if jordan:
            x_ref[...] = pltpu.roll(out, n - 8, 1)
            x_ref[at, :] = pltpu.roll(strip, n - 8, 1)
        else:
            x_ref[...] = pltpu.roll(jnp.where(ids >= 8, out, full), n - 8, 1)
            x_ref[at, :] = pltpu.roll(kept, n - 8, 1)
        return 0

    lax.fori_loop(0, n // 8, block, 0)


def piece(ref, k):
    parts, _, n = ref.shape
    rows = BAND // parts
    return ref[:, k * rows : (k + 1) * rows, :].reshape(BAND, n)


def whole(ref):
    parts, rows, n = ref.shape
    return ref[...].reshape(parts * rows, n)


def invert_chol(gram, cinv_ref, rinv_ref):
    n = BAND
    r = lax.broadcasted_iota(jnp.int32, (n, n), 0)
    c = lax.broadcasted_iota(jnp.int32, (n, n), 1)
    cinv_ref[...] = gram
    eliminate(cinv_ref, False)
    x = cinv_ref[...]
    diag = jnp.sum(jnp.where(r == c, x, 0.0), axis=1, keepdims=True)
    cinv = jnp.where(r > c, x, (r == c).astype(jnp.float32)) / jnp.sqrt(diag)
    cinv_ref[...] = cinv
    rinv_ref[...] = cinv.T


def invert_top(top, rinv_ref, f_ref, ft_ref, finv_ref, finvt_ref):
    n = BAND
    r = lax.broadcasted_iota(jnp.int32, (n, n), 0)
    c = lax.broadcasted_iota(jnp.int32, (n, n), 1)
    f = dot(top, rinv_ref[...]) + (r == c).astype(jnp.float32)
    f_ref[...] = f
    ft_ref[...] = f.T
    finv_ref[...] = f
    eliminate(finv_ref, True)
    finvt_ref[...] = finv_ref[...].T


def weights(fac, h, s_top, s_topt, a_ss):
    cinv, rinv, _, _, finv, finvt = fac
    half = dot(cinv, h) + s_top
    j = dot(half, rinv) + dot(cinv, s_topt) + a_ss
    return dot(dot(finv, j), finvt)


def step_one_kernel(
    pos_ref, cinv_ref, rinv_ref, f_ref, ft_ref, finv_ref, finvt_ref, h_ref, g_ref,
    pr_ref, sr_ref, er_ref, pc_ref, sc_ref, ec_ref, a_ref,
    updated_ref, p2r_ref, p2c_ref, t2_ref, a33_ref, left_ref, right_ref, ht_ref, zw_ref, small_ref,
):
    b = BAND
    n = pr_ref.shape[0]
    always = pos_ref[0] >= 0
    sums = lambda k: h_ref[k * b : (k + 1) * b, :]
    sumst = lambda k: ht_ref[:, k * b : (k + 1) * b]

    @pl.when(always)
    def _():
        for k in range(3):
            ht_ref[:, k * b : (k + 1) * b] = h_ref[k * b : (k + 1) * b, :].T

    a22, a31, a32, a33, a13, a23 = (functools.partial(piece, g_ref, k) for k in range(1, 7))

    @pl.when(always)
    def _():
        fac = tuple(ref[...] for ref in (cinv_ref, rinv_ref, f_ref, ft_ref, finv_ref, finvt_ref))
        small_ref[0, :, :] = weights(fac, sums(0), sums(1), sumst(1), a22())

    @pl.when(always)
    def _():
        small_ref[6, :, :] = dot(a31(), rinv_ref[...])
        small_ref[3, :, :] = dot(cinv_ref[...], a13())

    def work(slot, house, sums, cols):
        @pl.when(always)
        def _():
            rows = dot(dot(sums, rinv_ref[...]) + cols(), finvt_ref[...])
            small_ref[slot, :, :] = rows - 0.5 * dot(house(), small_ref[0])

    def workt(slot, house, sums, cols):
        @pl.when(always)
        def _():
            rows = dot(finv_ref[...], dot(cinv_ref[...], sums) + cols())
            small_ref[slot, :, :] = rows - 0.5 * dot(small_ref[0], house())

    work(5, lambda: small_ref[6], sums(2), a32)
    work(4, lambda: f_ref[...], sums(1), a22)
    workt(1, lambda: ft_ref[...], sumst(1), a22)
    workt(2, lambda: small_ref[3], sumst(2), a23)

    @pl.when(always)
    def _():
        zw_ref[:, 0:b] = small_ref[0]
        zw_ref[:, b : 2 * b] = small_ref[1]
        t2_ref[...] = a32() - dot(small_ref[6], small_ref[1]) - dot(small_ref[5], ft_ref[...])
        a33_ref[...] = a33() - dot(small_ref[6], small_ref[2]) - dot(small_ref[5], small_ref[3])

    tile = 2 * b if n % (2 * b) == 0 else b

    def side(start, p_ref, s_ref, e_ref, out_ref, house_at, work_at, p2_ref):
        @pl.loop(0, n // tile)
        def _(step):
            at = pl.ds(pl.multiple_of(step * tile, tile), tile)
            ids = start * n + step * tile + lax.broadcasted_iota(jnp.int32, (tile, b), 0)
            lane = lax.broadcasted_iota(jnp.int32, (tile, b), 1)
            house = dot(p_ref[at, :], rinv_ref[...]) + (ids - b == lane).astype(jnp.float32)
            cols = e_ref[at, :]
            both = dot(house, zw_ref[...])
            wk = dot(dot(s_ref[at, :], rinv_ref[...]) + cols, finvt_ref[...]) - 0.5 * both[:, :b]
            out_ref[at, house_at : house_at + b] = house
            out_ref[at, work_at : work_at + b] = wk
            p2 = cols - both[:, b:] - dot(wk, ft_ref[...])
            p2_ref[at, :] = jnp.where(ids >= 2 * b, p2, 0.0)

    side(pos_ref[0], pr_ref, sr_ref, er_ref, left_ref, 0, b, p2r_ref)
    side(pos_ref[1], pc_ref, sc_ref, ec_ref, right_ref, b, 0, p2c_ref)

    @pl.loop(0, n // tile)
    def _(step):
        at = pl.ds(pl.multiple_of(step * tile, tile), tile)
        updated_ref[at, :] = a_ref[at, :] - outer(left_ref[at, :], right_ref[...])


def step_two_kernel(
    pos_ref, cinv_ref, rinv_ref, f_ref, ft_ref, finv_ref, finvt_ref, h_ref, a33_ref,
    pr_ref, sr_ref, er_ref, pc_ref, sc_ref, ec_ref, a_ref,
    out_ref, left_ref, right_ref, ht_ref, z_ref, result_ref, sem,
):
    b = BAND
    n = pr_ref.shape[0]
    tile = 2 * b if n % (2 * b) == 0 else b

    @pl.when(pos_ref[0] >= 0)
    def _():
        ht_ref[...] = h_ref[b : 2 * b, :].T

    @pl.when(pos_ref[0] >= 0)
    def _():
        fac = tuple(ref[...] for ref in (cinv_ref, rinv_ref, f_ref, ft_ref, finv_ref, finvt_ref))
        z_ref[...] = weights(fac, h_ref[0:b, :], h_ref[b : 2 * b, :], ht_ref[...], a33_ref[...])

    def side(start, p_ref, s_ref, e_ref, out_ref, house_at, work_at):
        @pl.loop(0, n // tile)
        def _(step):
            at = pl.ds(pl.multiple_of(step * tile, tile), tile)
            ids = start * n + step * tile + lax.broadcasted_iota(jnp.int32, (tile, b), 0)
            lane = lax.broadcasted_iota(jnp.int32, (tile, b), 1)
            house = dot(p_ref[at, :], rinv_ref[...]) + (ids - 2 * b == lane).astype(jnp.float32)
            out_ref[at, house_at : house_at + b] = house
            ay = dot(s_ref[at, :], rinv_ref[...]) + e_ref[at, :]
            out_ref[at, work_at : work_at + b] = dot(ay, finvt_ref[...]) - 0.5 * dot(house, z_ref[...])

    side(pos_ref[0], pr_ref, sr_ref, er_ref, left_ref, 0, b)
    side(pos_ref[1], pc_ref, sc_ref, ec_ref, right_ref, b, 0)

    def store(step):
        at = pl.ds(pl.multiple_of(step * tile, tile), tile)
        return pltpu.make_async_copy(result_ref.at[at], out_ref.at[at], sem.at[step])

    @pl.loop(0, n // tile)
    def _(step):
        at = pl.ds(pl.multiple_of(step * tile, tile), tile)
        result_ref[at, :] = a_ref[at, :] - outer(left_ref[at, :], right_ref[...])
        store(step).start()

    @pl.loop(0, n // tile)
    def _(step):
        store(step).wait()


def call(body, outs, name, scratch, space=VMEM):
    def run(pos, *args):
        return pl.pallas_call(
            body,
            out_shape=tuple(jax.ShapeDtypeStruct(s, jnp.float32) for s in outs),
            in_specs=[pl.BlockSpec(memory_space=pltpu.SMEM)] + [pl.BlockSpec(memory_space=VMEM)] * len(args),
            out_specs=(pl.BlockSpec(memory_space=space),) * len(outs),
            scratch_shapes=scratch,
            name=name,
        )(pos, *args)

    return run


def greet(nr, nc, between=None):
    r, c = lax.axis_index("row"), lax.axis_index("col")
    barrier = pltpu.get_barrier_semaphore()
    for k in range(1, nc):
        pl.semaphore_signal(barrier, inc=1, device_id=(r, (c + k) % nc), device_id_type=MESH)
    for k in range(1, nr):
        pl.semaphore_signal(barrier, inc=1, device_id=((r + k) % nr, c), device_id_type=MESH)
    if between is not None:
        between(r, c)
    pl.semaphore_wait(barrier, nr + nc - 2)
    return r, c


def turn(a, block, out):
    for k in range(a.shape[1] // BAND):
        at = pl.ds(k * BAND, BAND)
        out[at, :] = a[pl.ds(block * BAND, BAND), at].T


def rows_at(index, size):
    return pl.ds(pl.multiple_of(index * size, 8), size)


class Spread:
    def __init__(self, axis, parts, me, other, dst, sems, pair_sems=None):
        self.pair = None if pair_sems is None else PairGather(me, other, parts, dst, pair_sems)
        self.axis, self.parts, self.me, self.other, self.dst = axis, parts, me, other, dst
        self.root_send, self.root_recv, self.send, self.recv = sems
        self.size = dst.shape[0] // parts

    def device(self, k):
        return (self.other, k) if self.axis == "col" else (k, self.other)

    def copy(self, k, src):
        rows = pl.ds(k * self.size, self.size)
        return pltpu.make_async_remote_copy(
            src_ref=src(rows),
            dst_ref=self.dst.at[rows],
            send_sem=self.root_send.at[k],
            recv_sem=self.root_recv,
            device_id=self.device(k),
            device_id_type=MESH,
        )

    def scatter(self, src):
        @pl.when(self.me == 0)
        def _():
            for k in range(1, self.parts):
                self.copy(k, src).start()
            rows = pl.ds(0, self.size)
            self.dst[rows, :] = src(rows)[...]

    def gather(self, src):
        @pl.when(self.me != 0)
        def _():
            self.copy(1, src).wait_recv()

        self.copies = []
        if self.pair is not None:
            self.pair.start()
            return
        for k in range(1, self.parts):
            rows = rows_at(self.me, self.size)
            copy = pltpu.make_async_remote_copy(
                src_ref=self.dst.at[rows],
                dst_ref=self.dst.at[rows],
                send_sem=self.send.at[k],
                recv_sem=self.recv.at[k],
                device_id=self.device((self.me + k) % self.parts),
                device_id_type=MESH,
            )
            copy.start()
            self.copies.append(copy)

    def finish(self, src):
        for copy in self.copies:
            copy.wait()
        if self.pair is not None:
            self.pair.finish()

        @pl.when(self.me == 0)
        def _():
            for k in range(1, self.parts):
                self.copy(k, src).wait_send()


class PairGather:
    def __init__(self, r, c, nr, dst, sems):
        self.r, self.c, self.count, self.dst = r, c, nr // 2, dst
        self.z, self.p = r // 2, r % 2
        self.sems = sems
        self.size = dst.shape[0] // nr

    def copy(self, src, index, to, stage, k):
        return pltpu.make_async_remote_copy(
            src_ref=src,
            dst_ref=self.dst.at[rows_at(index, self.size)],
            send_sem=self.sems[2 * stage].at[k],
            recv_sem=self.sems[2 * stage + 1].at[k],
            device_id=(to, self.c),
            device_id_type=MESH,
        )

    def start(self, src=None):
        src = self.dst.at[rows_at(self.r, self.size)] if src is None else src
        self.partner = 2 * self.z + 1 - self.p
        self.far = []
        for k in range(1, self.count):
            to = 2 * ((self.z + k) % self.count) + self.p
            self.far.append(self.copy(src, self.r, to, 0, k))
        for copy in self.far:
            copy.start()
        self.near = [self.copy(src, self.r, self.partner, 1, 0)]
        self.near[0].start()

    def forward(self):
        for k in sorted(range(1, self.count), key=lambda k: min(k, self.count - k)):
            self.far[k - 1].wait_recv()
            index = 2 * ((self.z + self.count - k) % self.count) + self.p
            copy = self.copy(self.dst.at[rows_at(index, self.size)], index, self.partner, 1, k)
            copy.start()
            self.near.append(copy)

    def finish(self):
        for copy in self.far:
            copy.wait_send()
        for copy in self.near:
            copy.wait()


def pair_sems(nr):
    return [pltpu.SemaphoreType.DMA((nr // 2,)) for _ in range(4)]


def spread_sems(parts):
    dma = pltpu.SemaphoreType.DMA
    return [dma((parts,)), dma, dma((parts,)), dma((parts,))]


def spread_kernel(nr, nc, a, pr, pc, ts, xr, xc, t, *sems):
    rows_sems, cols_sems, (send, recv, down_send, down_recv) = sems[:4], sems[4:8], sems[8:12]
    b = BAND

    def prepare(r, c):
        @pl.when(c == 0)
        def _():
            xr[...] = a[:, 0:b]

        @pl.when(r == 0)
        def _():
            turn(a, 0, xc)

        @pl.when((r == 0) & (c == 0))
        def _():
            xr[0:b, :] = jnp.zeros((b, b), jnp.float32)
            xc[0:b, :] = jnp.zeros((b, b), jnp.float32)
            rows = b // nc
            for k, (i, j) in enumerate(((1, 0), (1, 1), (2, 0), (2, 1), (2, 2), (0, 2), (1, 2))):
                block = a[i * b : (i + 1) * b, j * b : (j + 1) * b]
                t[:, k * rows : (k + 1) * rows, :] = block.reshape(nc, rows, b)

    r, c = greet(nr, nc, prepare)
    rows = Spread("col", nc, c, r, pr, rows_sems)
    cols = Spread("row", nr, r, c, pc, cols_sems, sems[12:])
    rows.scatter(lambda at: xr.at[at])
    cols.scatter(lambda at: xc.at[at])

    def slice_to(k):
        return pltpu.make_async_remote_copy(
            src_ref=t.at[k], dst_ref=ts, send_sem=send.at[k], recv_sem=recv, device_id=(r, k), device_id_type=MESH
        )

    def down(k):
        return pltpu.make_async_remote_copy(
            src_ref=ts, dst_ref=ts, send_sem=down_send.at[k], recv_sem=down_recv, device_id=(k, c), device_id_type=MESH
        )

    @pl.when((r == 0) & (c == 0))
    def _():
        for k in range(1, nc):
            slice_to(k).start()
        ts[...] = t[0]

    rows.gather(lambda at: xr.at[at])
    cols.gather(lambda at: xc.at[at])

    @pl.when((r == 0) & (c != 0))
    def _():
        slice_to(1).wait_recv()

    @pl.when(r == 0)
    def _():
        for k in range(1, nr):
            down(k).start()

    cols.pair.forward()

    @pl.when(r != 0)
    def _():
        down(1).wait_recv()

    rows.finish(lambda at: xr.at[at])
    cols.finish(lambda at: xc.at[at])

    @pl.when(r == 0)
    def _():
        for k in range(1, nr):
            down(k).wait_send()

    @pl.when((r == 0) & (c == 0))
    def _():
        for k in range(1, nc):
            slice_to(k).wait_send()


def middle_kernel(
    nr, nc, first, count, gather, a, pr, pc, t, cinv, rinv, f, ft, finv, finvt, out_r, out_c, out_h, er, ec, *rest
):
    out_t, rest = (rest[0], rest[1:]) if gather else (None, rest)
    sr, sc, h, gram, part_r, part_c, part_h, part_g, sum_r, sum_c, sum_h, sum_g, all_g, cols_h, all_h, xc, part_p, sum_p = rest[:18]
    send, recv, *sems = rest[18:]
    b = BAND
    n = a.shape[0]
    size_r, size_c, size_h, size_g = n // nc, n // nr, h.shape[0] // nc, b // nc

    def prepare(r, c):
        @pl.when(r >= 0)
        def _():
            gram[...] = mm(pr[...], pr[...], 0, 0)
            part_g[r] = gram[rows_at(c, size_g), :]

        @pl.when(r == 0)
        def _():
            turn(a, first, xc)

    r, c = greet(nr, nc, prepare)
    always = r >= 0

    def along(axis, phase, source, target):
        parts, me = (nc, c) if axis == "col" else (nr, r)
        copies = []
        for k in range(1, parts):
            to = (me + k) % parts
            copy = pltpu.make_async_remote_copy(
                src_ref=source(to),
                dst_ref=target(k),
                send_sem=send.at[phase, k],
                recv_sem=recv.at[phase, k],
                device_id=(r, to) if axis == "col" else (to, c),
                device_id_type=MESH,
            )
            copy.start()
            copies.append(copy)
        return copies

    sent = []

    def finish(copies):
        for copy in copies:
            copy.wait_recv()
        sent.extend(copies)

    def block(body):
        pl.when(always)(body)

    g_copies = along("row", 0, lambda to: gram.at[rows_at(c, size_g)], lambda k: part_g.at[r])
    rows = Spread("col", nc, c, r, er, sems[:4])
    cols = Spread("row", nr, r, c, ec, sems[4:8], sems[8:12])
    gather_c = PairGather(r, c, nr, out_c, sems[12:])
    rows_src = lambda at: a.at[at, first * b : (first + 1) * b]
    cols_src = lambda at: xc.at[at]
    rows.scatter(rows_src)
    cols.scatter(cols_src)

    tile = 2 * b if n % (2 * b) == 0 else b

    @pl.loop(0, n // tile)
    def _(step):
        at = pl.ds(pl.multiple_of(step * tile, tile), tile)
        sr[at, :] = dot(a[at, :], pc[...])

    @block
    def _():
        h[0:b, :] = mm(pr[...], sr[...], 0, 0)
        h[b : (1 + count) * b, :] = jnp.where(r == 0, sr[first * b : (first + count) * b, :], 0.0)

    finish(g_copies)
    value = part_g[0]
    for k in range(1, nr):
        value = value + part_g[k]
    sum_g[...] = value
    all_g[c] = value
    g_copies = along("col", 3, lambda to: sum_g, lambda k: all_g.at[c])
    h_copies = along("col", 4, lambda to: h.at[rows_at(to, size_h)], lambda k: part_h.at[k])
    r_copies = along("col", 2, lambda to: sr.at[rows_at(to, size_r)], lambda k: part_r.at[k])
    t_copies = []
    if gather:
        t_copies = along("col", 1, lambda to: t, lambda k: out_t.at[c])
        out_t[c] = t[...]

    @pl.loop(0, n // tile)
    def _(step):
        at = pl.ds(pl.multiple_of(step * tile, tile), tile)
        sc[at, :] = mm(a[:, at], pr[...], 0, 0)

    z, p = r // 2, r % 2
    half = nr // 2
    p_copies = []
    for i in range(half):
        copy = pltpu.make_async_remote_copy(
            src_ref=sc.at[rows_at(2 * i + 1 - p, size_c)],
            dst_ref=part_p.at[i],
            send_sem=send.at[5, i],
            recv_sem=recv.at[5, i],
            device_id=(2 * z + 1 - p, c),
            device_id_type=MESH,
        )
        copy.start()
        p_copies.append(copy)

    finish(h_copies)
    value = h[rows_at(c, size_h), :]
    for k in range(1, nc):
        value = value + part_h[k]
    sum_h[...] = value
    cols_h[r] = value
    h_copies = along("row", 6, lambda to: sum_h, lambda k: cols_h.at[r])

    finish(p_copies)
    for i in range(half):
        sum_p[i] = sc[rows_at(2 * i + p, size_c), :] + part_p[i]
    c_copies = []
    for k in range(1, half):
        to = (z + k) % half
        copy = pltpu.make_async_remote_copy(
            src_ref=sum_p.at[to],
            dst_ref=part_c.at[k],
            send_sem=send.at[8, k],
            recv_sem=recv.at[8, k],
            device_id=(2 * to + p, c),
            device_id_type=MESH,
        )
        copy.start()
        c_copies.append(copy)

    finish(r_copies)
    value = sr[rows_at(c, size_r), :]
    for k in range(1, nc):
        value = value + part_r[k]
    sum_r[...] = value
    out_r[rows_at(c, size_r), :] = value
    r_copies = along("col", 7, lambda to: sum_r, lambda k: out_r.at[rows_at(c, size_r)])
    rows.gather(rows_src)
    cols.gather(cols_src)
    finish(g_copies)

    @block
    def _():
        invert_chol(whole(all_g), cinv, rinv)

    finish(h_copies)
    value = cols_h[0]
    for k in range(1, nr):
        value = value + cols_h[k]
    all_h[...] = value
    out_h[rows_at(c, size_h), :] = value
    h_copies = along("col", 9, lambda to: all_h, lambda k: out_h.at[rows_at(c, size_h)])

    finish(c_copies)
    value = sum_p[z]
    for k in range(1, half):
        value = value + part_c[k]
    sum_c[...] = value
    out_c[rows_at(r, size_c), :] = value
    gather_c.start(sum_c)
    finish(t_copies)
    cols.pair.forward()

    @block
    def _():
        invert_top(piece(out_t, 0) if gather else t[...], rinv, f, ft, finv, finvt)

    gather_c.forward()
    for copies in (r_copies, h_copies):
        finish(copies)
    for copy in sent:
        copy.wait_send()
    gather_c.finish()
    rows.finish(rows_src)
    cols.finish(cols_src)


def spread(nr, nc, a):
    dma = pltpu.SemaphoreType.DMA
    b = BAND
    n = a.shape[0]
    tops = 7 * b // nc
    return pl.pallas_call(
        functools.partial(spread_kernel, nr, nc),
        out_shape=tuple(jax.ShapeDtypeStruct(s, jnp.float32) for s in ((n, b), (n, b), (tops, b))),
        in_specs=[pl.BlockSpec(memory_space=VMEM)],
        out_specs=(pl.BlockSpec(memory_space=VMEM),) * 3,
        scratch_shapes=[
            *(VMEM(s, jnp.float32) for s in ((n, b), (n, b), (nc, tops, b))),
            *spread_sems(nc), *spread_sems(nr), dma((nc,)), dma, dma((nr,)), dma, *pair_sems(nr),
        ],
        compiler_params=pltpu.CompilerParams(collective_id=0, has_side_effects=True),
        name="spread",
    )(a)


def middle(nr, nc, first, count, gather, a, pr, pc, t):
    most = max(nr, nc)
    dma = pltpu.SemaphoreType.DMA
    b = BAND
    n = a.shape[0]
    heads = (1 + count) * b
    size_r, size_c, size_h, size_g = n // nc, n // nr, heads // nc, b // nc
    outs = [(b, b)] * 6 + [(n, b), (n, b), (heads, b), (n, b), (n, b)]
    if gather:
        outs.append((nc, *t.shape))
    scratch = [
        (n, b), (n, b), (heads, b), (b, b),
        (nc, size_r, b), (nr // 2, size_c, b), (nc, size_h, b), (nr, size_g, b),
        (size_r, b), (size_c, b), (size_h, b), (size_g, b), (nc, size_g, b), (nr, size_h, b), (size_h, b), (n, b),
        (nr // 2, size_c, b), (nr // 2, size_c, b),
    ]
    return pl.pallas_call(
        functools.partial(middle_kernel, nr, nc, first, count, gather),
        out_shape=tuple(jax.ShapeDtypeStruct(s, jnp.float32) for s in outs),
        in_specs=[pl.BlockSpec(memory_space=VMEM)] * 4,
        out_specs=(pl.BlockSpec(memory_space=VMEM),) * len(outs),
        scratch_shapes=[
            *(VMEM(s, jnp.float32) for s in scratch),
            dma((10, most)), dma((10, most)),
            *spread_sems(nc), *spread_sems(nr), *pair_sems(nr), *pair_sems(nr),
        ],
        compiler_params=pltpu.CompilerParams(collective_id=first, has_side_effects=True),
        name=f"middle_{first}",
    )(a, pr, pc, t)


def shards(nr, nc, matrix):
    n = matrix.shape[0]
    b = BAND
    row, col = lax.axis_index("row"), lax.axis_index("col")
    pos = jnp.stack([row, col]).astype(jnp.int32)
    vmem = lambda *shape: VMEM(shape, jnp.float32)
    p1r, p1c, t = spread(nr, nc, matrix)
    *fac, sr, sc, h, er, ec, t = middle(nr, nc, 1, 2, True, matrix, p1r, p1c, t)
    one = call(
        step_one_kernel,
        [(n, n), (n, b), (n, b), (b, b), (b, b)],
        "step_one",
        [vmem(n, 2 * b), vmem(n, 2 * b), vmem(b, 3 * b), vmem(b, 2 * b), vmem(7, b, b)],
    )
    updated, p2r, p2c, t2, a33 = one(pos, *fac, h, t, p1r, sr, er, p1c, sc, ec, matrix)
    *fac, sr, sc, h, er, ec = middle(nr, nc, 2, 1, False, updated, p2r, p2c, t2)
    two = call(
        step_two_kernel,
        [(n, n)],
        "step_two",
        [vmem(n, 2 * b), vmem(n, 2 * b), vmem(b, b), vmem(b, b), vmem(n, n), pltpu.SemaphoreType.DMA((n // b,))],
        pl.ANY,
    )
    return two(pos, *fac, h, a33, p2r, sr, er, p2c, sc, ec, updated)[0]


def solution(mesh):
    spec = P("row", "col")
    body = functools.partial(shards, mesh.shape["row"], mesh.shape["col"])
    return jax.shard_map(body, mesh=mesh, in_specs=(spec,), out_specs=spec, check_vma=False)
```
